256 devices in a mesh: tile: 64 (over x, z, core), mode: 4 (over y).
Axes of the slice: x: 4, y: 4, z: 8, core: 2. Of those that a mesh axis runs over, the one named last changes fastest.
Arguments:
- object_tiles: bfloat16 [64, 2, 2, 256, 256], P('tile'), may hold values from -4 to 4
- probes: float32 [4, 2, 256, 256], P('mode'), may hold values from -4 to 4
- measured: bfloat16 [64, 8, 256, 256], P('tile'), may hold values from 0.25 to 4
- offsets: int32 [64, 8, 2], P('tile'), may hold values from 0 to 255, as said below
- counts: int32 [64], P('tile'), may hold values from 1 to 8, 320 in all
Outputs:
- object_grad: float32 [64, 2, 2, 256, 256], P('tile', None, None, 'mode')
- probe_grad: float32 [4, 2, 256, 256], P('mode')
The draws below stay inside these ranges and needn't reach their ends.
Inputs may be any that keep to these rules, and one draw needn't show every extreme that they name: Slots 0 .. counts[t] - 1 of tile t hold scan positions; the others are empty. Some tile has 8 live slots. Row offsets lie in 0 .. 255 and column offsets in 128 .. 255.
All inputs are finite; a program needn't handle non-finite values. No bound on the sum of `counts` on one device may be relied on, other than what follows from the above.
Results may differ from the reference program's by a relative error of at most 0.019.
Values may be sent and summed in bfloat16 or wider, within the bound.
No kernel may reach another device: no remote copies, remote signals or barrier semaphores. Data moves between devices by JAX's collectives and lax.ppermute only.
A program may use at most 128 MiB of HBM per device.

```python
import math
import jax
import jax.numpy as jnp
import numpy as np
from jax import lax

PW = 256
MODES = 4
SLICES = 2
TS = 256
TGX = 8
SLOTS = 8
TILES = 64


def draw_offsets(key, part):
    row_key = jax.random.fold_in(key, 11)
    col_key = jax.random.fold_in(key, 23)
    row_values = jax.random.randint(row_key, (TILES, SLOTS, 1), 0, TS, dtype=jnp.int32)
    col_values = jax.random.randint(col_key, (TILES, SLOTS, 1), TS // 2, TS, dtype=jnp.int32)
    return jnp.concatenate([row_values, col_values], axis=2)


def level_of(stream_key, shape, split, low, high):
    loudness, own = 1.0, jax.random.fold_in(stream_key, 6)
    for axis_at, shards_of in split:
        heights = jnp.exp(jax.random.uniform(jax.random.fold_in(own, axis_at), (shards_of,), jnp.float32, low / len(split), high / len(split)))
        loudness = loudness * jnp.repeat(heights, shape[axis_at] // shards_of).reshape([-1 if axis == axis_at else 1 for axis in range(len(shape))])
    return loudness


def profile(amount, total, most, slope):
    loads = [(1 << 20) // math.isqrt(standing ** slope) + 1 for standing in range(2, amount + 1)]
    spare, given = total - most - (amount - 1), [1] * (amount - 1)
    while spare > 0:
        movable = [i for i in range(amount - 1) if given[i] < most]
        whole, left = sum([loads[i] for i in movable]), spare
        for i in movable:
            more = min(most - given[i], max(1, left * loads[i] // whole), spare)
            given[i] = given[i] + more
            spare = spare - more
    return np.array([most] + given)


def uneven_parts(own_key, number_of, total, most, lean):
    if number_of == 2:
        one = jax.random.randint(own_key, (), max(1, total - most), min(most, total - 1) + 1)
        return jnp.stack([one, total - one])
    lengths = jnp.asarray(profile(number_of, total, most, lean), jnp.int32)
    couples = (number_of - 1) // 2
    giver, taker = lengths[1:1 + 2 * couples:2], lengths[2:2 + 2 * couples:2]
    room = jnp.minimum(giver - 1, most - taker)
    shifted = jax.random.randint(jax.random.fold_in(own_key, 1), (couples,), 0, 1 << 20) % (room + 1)
    lengths = lengths.at[1:1 + 2 * couples:2].set(giver - shifted).at[2:2 + 2 * couples:2].set(taker + shifted)
    return lengths[jax.random.permutation(jax.random.fold_in(own_key, 2), number_of)]


def noise(own_key, shape, spread, most, shards=(), kind=jnp.bfloat16):
    values = jax.random.normal(own_key, shape, jnp.float32) * spread
    if len(shards) > 0:
        values = level_of(own_key, shape, shards, -0.22, 0.18) * values
    return jnp.clip(values, min=-most, max=most).astype(kind)


def setup_inputs(seed: int = 0) -> dict:
    splits = jax.random.split(jax.random.key(seed), 6)
    object_tiles = noise(splits[0], (TILES, SLICES, 2, TS, TS), 0.6, 4.0, ((0, 64),))
    probes = noise(splits[1], (MODES, 2, PW, PW), 0.5, 4.0, ((0, 4),), jnp.float32)
    measured = jnp.clip(jnp.exp(math.log(4.0) - 2.7725887 * jax.random.uniform(splits[2], (TILES, SLOTS, PW, PW), jnp.float32) ** level_of(splits[2], (TILES, SLOTS, PW, PW), ((0, 64),), -0.2, 0.2)), 0.25, 4.0).astype(jnp.bfloat16)
    offsets = draw_offsets(jax.random.fold_in(splits[5], 71), 0)
    counts = uneven_parts(splits[4], TILES, TILES * SLOTS * 5 // 8, SLOTS, 2).astype(jnp.int32)
    return dict(object_tiles=object_tiles, probes=probes, measured=measured, offsets=offsets, counts=counts)


def fourier_tables(extent):
    indices = jnp.arange(extent, dtype=jnp.int32)
    products = indices[:, None] * indices[None, :] % extent
    angles = products.astype(jnp.float32) * (2.0 * math.pi / extent)
    factor = 1.0 / math.sqrt(extent)
    return ((jnp.cos(angles) * factor).astype(jnp.bfloat16), (jnp.sin(angles) * factor).astype(jnp.bfloat16))

def fresnel_kernel(extent):
    indices = jnp.arange(extent, dtype=jnp.int32)
    frequency = ((indices + extent // 2) % extent - extent // 2).astype(jnp.float32) / extent
    squared = frequency[:, None] * frequency[:, None] + frequency[None, :] * frequency[None, :]
    angles = squared * (-math.pi * extent / 8.0)
    return (jnp.cos(angles), jnp.sin(angles))

def times_complex(left_factor, right_factor):
    return (left_factor[0] * right_factor[0] - left_factor[1] * right_factor[1], left_factor[0] * right_factor[1] + left_factor[1] * right_factor[0])

def times_conjugate(left_factor, right_factor):
    return (left_factor[0] * right_factor[0] + left_factor[1] * right_factor[1], left_factor[0] * right_factor[1] - left_factor[1] * right_factor[0])

def rounded_copy(values):
    return lax.optimization_barrier(values.astype(jnp.bfloat16)).astype(jnp.float32)

def matmul_left(table, values):
    return jnp.einsum('jk,...kl->...jl', table.astype(jnp.float32), values, precision=lax.Precision.HIGHEST)

def matmul_right(values, table):
    return jnp.einsum('...jk,kl->...jl', values, table.astype(jnp.float32), precision=lax.Precision.HIGHEST)

def fourier_apply(wavefield, cosine_table, sine_table, signum):
    real_in = rounded_copy(wavefield[0])
    imag_in = rounded_copy(wavefield[1])
    middle_real = matmul_left(cosine_table, real_in) + signum * matmul_left(sine_table, imag_in)
    middle_imag = matmul_left(cosine_table, imag_in) - signum * matmul_left(sine_table, real_in)
    real_in = rounded_copy(middle_real)
    imag_in = rounded_copy(middle_imag)
    return (matmul_right(real_in, cosine_table) + signum * matmul_right(imag_in, sine_table), matmul_right(imag_in, cosine_table) - signum * matmul_right(real_in, sine_table))

def forward_pass(slice_one, slice_two, modes_pair, tables_all):
    cosine_table, sine_table, kernel = tables_all
    wave_one = times_complex(modes_pair, slice_one)
    spectrum = fourier_apply(wave_one, cosine_table, sine_table, 1.0)
    spectrum = times_complex(spectrum, kernel)
    arrived = fourier_apply(spectrum, cosine_table, sine_table, -1.0)
    wave_two = times_complex(slice_two, arrived)
    farfield = fourier_apply(wave_two, cosine_table, sine_table, 1.0)
    return (arrived, farfield)

def backward_pass(slice_one, slice_two, modes_pair, arrived, far_grad, tables_all):
    cosine_table, sine_table, kernel = tables_all
    exit_grad = fourier_apply(far_grad, cosine_table, sine_table, -1.0)
    second_grad = times_conjugate(arrived, exit_grad)
    arrived_grad = times_conjugate(slice_two, exit_grad)
    spectrum_grad = fourier_apply(arrived_grad, cosine_table, sine_table, 1.0)
    spectrum_grad = times_conjugate(kernel, spectrum_grad)
    wave_grad = fourier_apply(spectrum_grad, cosine_table, sine_table, -1.0)
    first_grad = times_conjugate(modes_pair, wave_grad)
    probe_term = times_conjugate(slice_one, wave_grad)
    return (first_grad, second_grad, probe_term)

def reference(object_tiles, probes, measured, offsets, counts):
    cosine_table, sine_table = fourier_tables(PW)
    tables_all = (cosine_table, sine_table, fresnel_kernel(PW))
    extra = TGX + 1
    padded = jnp.concatenate([object_tiles, jnp.zeros((extra, SLICES, 2, TS, TS), jnp.bfloat16)], axis=0)
    modes_pair = (probes[None, :, 0], probes[None, :, 1])
    zero_start = jnp.zeros((), jnp.int32)

    def one_tile(carry, inputs):
        grad_tiles, probe_total = carry
        tile_index, tile_offsets, tile_count, tile_measured = inputs

        def take(index):
            return lax.dynamic_index_in_dim(padded, index, 0, keepdims=False)
        upper = jnp.concatenate([take(tile_index), take(tile_index + 1)], axis=-1)
        lower = jnp.concatenate([take(tile_index + TGX), take(tile_index + TGX + 1)], axis=-1)
        window = jnp.concatenate([upper, lower], axis=-2)

        def cut_patch(row_start, col_start):
            return lax.dynamic_slice(window, (zero_start, zero_start, row_start, col_start), (SLICES, 2, PW, PW))
        patches = jax.vmap(cut_patch)(tile_offsets[:, 0], tile_offsets[:, 1]).astype(jnp.float32)
        slice_one = (patches[:, 0, 0][:, None], patches[:, 0, 1][:, None])
        slice_two = (patches[:, 1, 0][:, None], patches[:, 1, 1][:, None])
        arrived, farfield = forward_pass(slice_one, slice_two, modes_pair, tables_all)
        intensity = lax.optimization_barrier(jnp.sum(farfield[0] * farfield[0] + farfield[1] * farfield[1], axis=1))
        live = (jnp.arange(SLOTS, dtype=jnp.int32) < tile_count).astype(jnp.float32)
        weight = (live[:, None, None] * (intensity - tile_measured.astype(jnp.float32)))[:, None]
        far_grad = (weight * farfield[0], weight * farfield[1])
        first_grad, second_grad, probe_term = backward_pass(slice_one, slice_two, modes_pair, arrived, far_grad, tables_all)
        first_sum = jnp.stack([lax.optimization_barrier(jnp.sum(first_grad[0], axis=1)), lax.optimization_barrier(jnp.sum(first_grad[1], axis=1))], axis=1)
        second_sum = jnp.stack([lax.optimization_barrier(jnp.sum(second_grad[0], axis=1)), lax.optimization_barrier(jnp.sum(second_grad[1], axis=1))], axis=1)
        patch_grad = jnp.stack([first_sum, second_sum], axis=1)

        def place(slot, accum):
            start = (zero_start, zero_start, tile_offsets[slot, 0], tile_offsets[slot, 1])
            current = lax.dynamic_slice(accum, start, (SLICES, 2, PW, PW))
            return lax.dynamic_update_slice(accum, current + patch_grad[slot], start)
        window_grad = lax.fori_loop(0, SLOTS, place, jnp.zeros((SLICES, 2, 2 * TS, 2 * TS), jnp.float32))

        def add_quarter(accum, index, quarter):
            current = lax.dynamic_index_in_dim(accum, index, 0, keepdims=True)
            return lax.dynamic_update_index_in_dim(accum, current + quarter[None], index, 0)
        grad_tiles = add_quarter(grad_tiles, tile_index, window_grad[:, :, :TS, :TS])
        grad_tiles = add_quarter(grad_tiles, tile_index + 1, window_grad[:, :, :TS, TS:])
        grad_tiles = add_quarter(grad_tiles, tile_index + TGX, window_grad[:, :, TS:, :TS])
        grad_tiles = add_quarter(grad_tiles, tile_index + TGX + 1, window_grad[:, :, TS:, TS:])
        probe_total = probe_total + jnp.stack([lax.optimization_barrier(jnp.sum(probe_term[0], axis=0)), lax.optimization_barrier(jnp.sum(probe_term[1], axis=0))], axis=1)
        return ((grad_tiles, probe_total), None)
    start_grad = jnp.zeros((TILES + extra, SLICES, 2, TS, TS), jnp.float32)
    start_probe = jnp.zeros((MODES, 2, PW, PW), jnp.float32)
    tile_numbers = jnp.arange(TILES, dtype=jnp.int32)
    (grad_tiles, probe_total), _ = lax.scan(one_tile, (start_grad, start_probe), (tile_numbers, offsets, counts, measured))
    return (grad_tiles[:TILES], probe_total)
```

```python
import math

import jax
import jax.numpy as jnp
import numpy as np
from jax import lax
from jax.experimental import pallas as pl
from jax.experimental.pallas import tpu as pltpu
from jax.sharding import PartitionSpec as P

PW = 256
HALF = 128
SLOTS = 8
MODES = 4
TGX = 8
TILES = 64
SHARE = PW // MODES
f32 = jnp.float32
bf16 = jnp.bfloat16


def constants():
    indices = np.arange(PW)
    angles = ((indices[:, None] * indices[None, :]) % PW) * (2.0 * math.pi / PW)
    cosine = (np.cos(angles) / math.sqrt(PW)).astype(bf16)
    sine = (np.sin(angles) / math.sqrt(PW)).astype(bf16)
    frequency = (((indices + PW // 2) % PW) - PW // 2) / PW
    phase = np.exp(-1j * math.pi * (PW / 8.0) * frequency * frequency)
    table = cosine.astype(np.float64) - 1j * sine.astype(np.float64)
    hop = np.conj(table) @ (phase[:, None] * table)
    hop_real = hop.real.astype(bf16)
    hop_imag = hop.imag.astype(bf16)
    return (
        np.block([[cosine, sine], [-sine, cosine]]),
        np.block([[cosine, -sine], [sine, cosine]]),
        np.block([[hop_real, -hop_imag], [hop_imag, hop_real]]),
        np.block([[hop_real, hop_imag], [-hop_imag, hop_real]]),
    )


def dot(left, right):
    return jnp.dot(left, right, preferred_element_type=f32)


def build_window(window, own, east, south, corner):
    for part in range(2):
        window[part, 0, 0:PW] = own[part, :, HALF:].astype(f32)
        window[part, 0, PW:] = south[part].astype(f32)
        for lane_tile in range(2):
            lanes = slice(HALF * lane_tile, HALF * lane_tile + HALF)
            window[part, 1 + lane_tile, 0:PW] = east[part, :, lanes].astype(f32)
            window[part, 1 + lane_tile, PW:] = corner[part, :, lanes].astype(f32)


def corner_of(meta, turn):
    slot = meta[2 * SLOTS + 1] + MODES * turn
    return meta[2 * slot], meta[2 * slot + 1] - HALF, slot < meta[2 * SLOTS]


def cut(window, patch, row, col):
    keep = lax.broadcasted_iota(jnp.int32, (64, HALF), 1) < HALF - col
    turn = jnp.where(col == 0, 0, HALF - col)
    for part in range(2):
        for block in range(4):
            rows = pl.ds(row + 64 * block, 64)
            rolled = [pltpu.roll(window[part, t, rows], turn, 1) for t in range(3)]
            at = slice(64 * block, 64 * block + 64)
            patch[part, at, 0:HALF] = jnp.where(keep, rolled[0], rolled[1])
            patch[part, at, HALF:PW] = jnp.where(keep, rolled[1], rolled[2])


def place(total, patch, row, col):
    low = lax.broadcasted_iota(jnp.int32, (64, HALF), 1) < col
    zero = jnp.zeros((64, HALF), f32)
    for part in range(2):
        for block in range(4):
            rows = pl.ds(row + 64 * block, 64)
            at = slice(64 * block, 64 * block + 64)
            left = pltpu.roll(patch[part, at, 0:HALF], col, 1)
            right = pltpu.roll(patch[part, at, HALF:PW], col, 1)
            total[part, 0, rows] = total[part, 0, rows] + jnp.where(low, zero, left)
            total[part, 1, rows] = total[part, 1, rows] + jnp.where(low, left, right)
            total[part, 2, rows] = total[part, 2, rows] + jnp.where(low, right, zero)


def share_rows(total, shares, mode):
    for step in range(MODES):
        owner = lax.rem(mode + step, MODES)
        for half in range(2):
            rows = pl.ds(pl.multiple_of(PW * half + SHARE * owner, SHARE), SHARE)
            for part in range(2):
                for t in range(3):
                    shares[step][part, half, t] = total[part, t, rows].astype(bf16)


def set_rows(both, top, bottom):
    both[0:PW] = top.astype(bf16)
    both[PW:] = bottom.astype(bf16)


def set_lanes(both, stacked):
    both[:, 0:PW] = stacked[0:PW].astype(bf16)
    both[:, PW:] = stacked[PW:].astype(bf16)


def propagate_kernel(meta, own, east, south, corner, p0, p1, p2, p3, left, right, arrived, window, patch, probes, rows, lanes):
    for mode, probe in enumerate((p0, p1, p2, p3)):
        probes[mode] = probe[...]
    build_window(window, own, east, south, corner)

    def one_slot(turn, _):
        row, col, _live = corner_of(meta, turn)
        cut(window, patch, row, col)

        def one_mode(mode, _):
            probe_real, probe_imag = probes[mode, 0].astype(f32), probes[mode, 1].astype(f32)
            real, imag = patch[0], patch[1]
            set_rows(rows, probe_real * real - probe_imag * imag, probe_real * imag + probe_imag * real)
            set_lanes(lanes, dot(left[...], rows[...]))
            arrived[turn, mode] = dot(lanes[...], right[...])
            return 0

        return lax.fori_loop(0, MODES, one_mode, 0)

    lax.fori_loop(0, 2, one_slot, 0)


def detector_kernel(meta, own, east, south, corner, arrived, measured, plus, minus, arrived_grad, g0, g1, g2, g3, window, patch, rows, lanes, far, weight, second, total):
    build_window(window, own, east, south, corner)
    total[...] = jnp.zeros_like(total)

    def one_slot(turn, _):
        row, col, live = corner_of(meta, turn)
        cut(window, patch, row, col)

        def forth(mode, _):
            wave_real, wave_imag = arrived[turn, mode, :, 0:PW], arrived[turn, mode, :, PW:]
            real, imag = patch[0], patch[1]
            set_rows(rows, wave_real * real - wave_imag * imag, wave_real * imag + wave_imag * real)
            set_lanes(lanes, dot(plus[...], rows[...]))
            field = dot(lanes[...], minus[...])
            far[mode] = field
            power = field[:, 0:PW] * field[:, 0:PW] + field[:, PW:] * field[:, PW:]

            @pl.when(mode == 0)
            def _():
                weight[...] = power - measured[turn].astype(f32)

            @pl.when(mode > 0)
            def _():
                weight[...] = weight[...] + power

            return 0

        lax.fori_loop(0, MODES, forth, 0)
        weight[...] = jnp.where(live, weight[...], 0.0)
        second[...] = jnp.zeros_like(second)

        def back(mode, _):
            scale = weight[...]
            set_rows(rows, scale * far[mode, :, 0:PW], scale * far[mode, :, PW:])
            set_lanes(lanes, dot(minus[...], rows[...]))
            leaving = dot(lanes[...], plus[...])
            grad_real, grad_imag = leaving[:, 0:PW], leaving[:, PW:]
            wave_real, wave_imag = arrived[turn, mode, :, 0:PW], arrived[turn, mode, :, PW:]
            second[0] = second[0] + (wave_real * grad_real + wave_imag * grad_imag)
            second[1] = second[1] + (wave_real * grad_imag - wave_imag * grad_real)
            real, imag = patch[0], patch[1]
            arrived_grad[turn, mode, 0:PW] = (real * grad_real + imag * grad_imag).astype(bf16)
            arrived_grad[turn, mode, PW:] = (real * grad_imag - imag * grad_real).astype(bf16)
            return 0

        lax.fori_loop(0, MODES, back, 0)
        place(total, second, row, col)
        return 0

    lax.fori_loop(0, 2, one_slot, 0)
    share_rows(total, (g0, g1, g2, g3), meta[2 * SLOTS + 1])


def return_kernel(meta, own, east, south, corner, arrived_grad, p0, p1, p2, p3, left, right, g0, g1, g2, g3, kept, sent, window, patch, probes, lanes, first, total, probe_total):
    for mode, probe in enumerate((p0, p1, p2, p3)):
        probes[mode] = probe[...]
    build_window(window, own, east, south, corner)
    total[...] = jnp.zeros_like(total)
    probe_total[...] = jnp.zeros_like(probe_total)

    def one_slot(turn, _):
        row, col, _live = corner_of(meta, turn)
        cut(window, patch, row, col)
        first[...] = jnp.zeros_like(first)

        def one_mode(mode, _):
            set_lanes(lanes, dot(left[...], arrived_grad[turn, mode]))
            grad = dot(lanes[...], right[...])
            grad_real, grad_imag = grad[:, 0:PW], grad[:, PW:]
            probe_real, probe_imag = probes[mode, 0].astype(f32), probes[mode, 1].astype(f32)
            real, imag = patch[0], patch[1]
            first[0] = first[0] + (probe_real * grad_real + probe_imag * grad_imag)
            first[1] = first[1] + (probe_real * grad_imag - probe_imag * grad_real)
            probe_total[0, mode] = probe_total[0, mode] + (real * grad_real + imag * grad_imag)
            probe_total[1, mode] = probe_total[1, mode] + (real * grad_imag - imag * grad_real)
            return 0

        lax.fori_loop(0, MODES, one_mode, 0)
        place(total, first, row, col)
        return 0

    lax.fori_loop(0, 2, one_slot, 0)
    share_rows(total, (g0, g1, g2, g3), meta[2 * SLOTS + 1])
    core = meta[2 * SLOTS + 2]
    kept[...] = probe_total[core]
    sent[...] = probe_total[1 - core].astype(bf16)


def kernel_call(body, out_shape, scratch, name, operands, flops):
    vmem = pl.BlockSpec(memory_space=pltpu.VMEM)
    smem = pl.BlockSpec(memory_space=pltpu.SMEM)
    return pl.pallas_call(
        body,
        out_shape=tuple(jax.ShapeDtypeStruct(*shape) for shape in out_shape),
        in_specs=[smem] + [vmem] * (len(operands) - 1),
        out_specs=tuple(vmem for _ in out_shape),
        scratch_shapes=[pltpu.VMEM(*shape) for shape in scratch],
        compiler_params=pltpu.CompilerParams(vmem_limit_bytes=48 << 20),
        cost_estimate=pl.CostEstimate(flops=flops, bytes_accessed=12 << 20, transcendentals=0),
        name=name,
    )(*operands)


WINDOW = ((2, 3, 2 * PW, HALF), f32)
PATCH = ((2, PW, PW), f32)
ROWS = ((2 * PW, PW), bf16)
LANES = ((PW, 2 * PW), bf16)
PROBES = ((MODES, 2, PW, PW), bf16)
SHARES = [((2, 2, 3, SHARE, HALF), bf16)] * MODES
TRANSFORM = 8 * 16 * PW * PW * PW


def toward(value, steps):
    pairs = [(t, t + steps) for t in range(TILES) if 0 <= t + steps < TILES]
    return lax.ppermute(value, "tile", pairs)


def to_mode(value, steps):
    return lax.ppermute(value, "mode", [(m, (m + steps) % MODES) for m in range(MODES)])


def tile_of(x, z, core):
    return (x * 8 + z) * 2 + core


def along_x(value, steps):
    pairs = [(tile_of(x, z, c), tile_of((x + steps) % 4, z, c)) for x in range(4) for z in range(8) for c in range(2)]
    return lax.ppermute(value, "tile", pairs)


def along_z(value, steps):
    pairs = [(tile_of(x, z, c), tile_of(x, (z + steps) % 8, c)) for x in range(4) for z in range(8) for c in range(2)]
    return lax.ppermute(value, "tile", pairs)


def to_core(value):
    return lax.ppermute(value, "tile", [(t, t ^ 1) for t in range(TILES)])


def own_rows(shares):
    total = shares[0].astype(f32)
    for step in range(1, MODES):
        total = total + to_mode(shares[step], step).astype(f32)
    return total


def own_tile(total):
    eastward = toward(total[:, :, 1:].astype(bf16), 1).astype(f32)
    first = total[:, :, 0]
    joined = jnp.concatenate([eastward[:, :, 0], eastward[:, :, 1] + first], axis=-1)
    southward = toward(joined[:, 1].astype(bf16), TGX).astype(f32)
    return joined[:, 0] + southward


def probe_sum(kept, sent, core, x, z):
    total = kept + to_core(sent).astype(f32)
    mine = total[0]
    for step in range(1, MODES):
        mine = mine + to_mode(total[step].astype(bf16), step).astype(f32)
    quarters = mine.reshape(4, 64, PW)

    def quarter(step):
        return lax.dynamic_index_in_dim(quarters, lax.rem(x + step, 4), 0, keepdims=False)

    part = quarter(0)
    for step in range(1, 4):
        part = part + along_x(quarter(step).astype(bf16), step).astype(f32)
    part = part.astype(bf16)
    gathered = jnp.stack([part] + [along_z(part, 8 - step) for step in range(1, 8)])
    gathered = jnp.roll(gathered, z, axis=0)
    whole = jnp.sum(gathered.astype(f32), axis=0).astype(bf16)
    pieces = jnp.stack([whole] + [along_x(whole, 4 - step) for step in range(1, 4)])
    plane = jnp.roll(pieces, x, axis=0).reshape(PW, PW)
    other = to_core(plane)
    real = jnp.where(core == 0, plane, other)
    imag = jnp.where(core == 0, other, plane)
    return jnp.stack([real, imag]).astype(f32)


def shards(object_tiles, probes, measured, offsets, counts):
    plus, minus, left, right = (jnp.asarray(matrix) for matrix in constants())
    tile = lax.axis_index("tile")
    mode = lax.axis_index("mode")
    core, z, x = lax.rem(tile, 2), lax.rem(tile // 2, 8), tile // 16
    meta = jnp.concatenate([offsets.reshape(-1), counts, jnp.stack([mode, core])]).astype(jnp.int32)
    pieces = []
    for depth in range(2):
        own = object_tiles[0, depth]
        pieces.append((own, toward(own, -1), toward(own[:, :, HALF:], -TGX), toward(own, -TGX - 1)))
        if depth == 0:
            probe = probes[0].astype(bf16)
            all_probes = [probe] + [to_mode(probe, MODES - step) for step in range(1, MODES)]
    turns = lax.dynamic_index_in_dim(measured[0].reshape(2, MODES, PW, PW), mode, 1, keepdims=False)

    (arrived,) = kernel_call(
        propagate_kernel,
        [((2, MODES, PW, 2 * PW), f32)],
        [WINDOW, PATCH, PROBES, ROWS, LANES],
        "propagate",
        (meta, *pieces[0], *all_probes, left, right),
        TRANSFORM,
    )
    arrived_grad, *second_shares = kernel_call(
        detector_kernel,
        [((2, MODES, 2 * PW, PW), bf16)] + SHARES,
        [WINDOW, PATCH, ROWS, LANES, ((MODES, PW, 2 * PW), f32), ((PW, PW), f32), PATCH, WINDOW],
        "detector",
        (meta, *pieces[1], arrived, turns, plus, minus),
        2 * TRANSFORM,
    )
    second = own_tile(own_rows(second_shares))
    *first_shares, kept, sent = kernel_call(
        return_kernel,
        SHARES + [((MODES, PW, PW), f32), ((MODES, PW, PW), bf16)],
        [WINDOW, PATCH, PROBES, LANES, PATCH, WINDOW, ((2, MODES, PW, PW), f32)],
        "returned",
        (meta, *pieces[0], arrived_grad, *all_probes, right, left),
        TRANSFORM,
    )
    probe_grad = probe_sum(kept, sent, core, x, z)
    first = own_tile(own_rows(first_shares))
    return (jnp.stack([first, second])[None], probe_grad[None])


def solution(mesh):
    placed = (
        P("tile", None, None, None, None),
        P("mode", None, None, None),
        P("tile", None, None, None),
        P("tile", None, None),
        P("tile"),
    )
    return jax.shard_map(
        shards,
        mesh=mesh,
        in_specs=placed,
        out_specs=(P("tile", None, None, "mode", None), P("mode", None, None, None)),
        check_vma=False,
    )
```

```python
import math

import jax
import jax.numpy as jnp
import numpy as np
from jax import lax
from jax.experimental import pallas as pl
from jax.experimental.pallas import tpu as pltpu
from jax.sharding import PartitionSpec as P

PW = 256
HALF = 128
SLOTS = 8
MODES = 4
TGX = 8
TILES = 64
SHARE = PW // MODES
UNROLL = 4
f32 = jnp.float32
bf16 = jnp.bfloat16


def constants():
    indices = np.arange(PW)
    angles = ((indices[:, None] * indices[None, :]) % PW) * (2.0 * math.pi / PW)
    cosine = (np.cos(angles) / math.sqrt(PW)).astype(bf16)
    sine = (np.sin(angles) / math.sqrt(PW)).astype(bf16)
    frequency = (((indices + PW // 2) % PW) - PW // 2) / PW
    phase = np.exp(-1j * math.pi * (PW / 8.0) * frequency * frequency)
    table = cosine.astype(np.float64) - 1j * sine.astype(np.float64)
    hop = np.conj(table) @ (phase[:, None] * table)
    hop_real = hop.real.astype(bf16)
    hop_imag = hop.imag.astype(bf16)
    return cosine, sine, hop_real, hop_imag


def block_forms(cosine, sine, hop_real, hop_imag):
    return (
        jnp.block([[cosine, sine], [-sine, cosine]]),
        jnp.block([[cosine, -sine], [sine, cosine]]),
        jnp.block([[hop_real, -hop_imag], [hop_imag, hop_real]]),
        jnp.block([[hop_real, hop_imag], [-hop_imag, hop_real]]),
    )


def dot(left, right):
    return jnp.dot(left, right, preferred_element_type=f32)


def build_window(window, own, east, south, corner):
    for part in range(2):
        window[part, 0, 0:PW] = own[part, :, HALF:].astype(f32)
        window[part, 0, PW:] = south[part].astype(f32)
        for lane_tile in range(2):
            lanes = slice(HALF * lane_tile, HALF * lane_tile + HALF)
            window[part, 1 + lane_tile, 0:PW] = east[part, :, lanes].astype(f32)
            window[part, 1 + lane_tile, PW:] = corner[part, :, lanes].astype(f32)


def corner_of(meta, turn):
    slot = meta[2 * SLOTS + 1] + MODES * turn
    return meta[2 * slot], meta[2 * slot + 1] - HALF, slot < meta[2 * SLOTS]


def cut(window, patch, row, col):
    keep = lax.broadcasted_iota(jnp.int32, (64, HALF), 1) < HALF - col
    turn = jnp.where(col == 0, 0, HALF - col)
    for part in range(2):
        for block in range(4):
            rows = pl.ds(row + 64 * block, 64)
            rolled = [pltpu.roll(window[part, t, rows], turn, 1) for t in range(3)]
            at = slice(64 * block, 64 * block + 64)
            patch[part, at, 0:HALF] = jnp.where(keep, rolled[0], rolled[1])
            patch[part, at, HALF:PW] = jnp.where(keep, rolled[1], rolled[2])


def place(total, patch, row, col):
    low = lax.broadcasted_iota(jnp.int32, (64, HALF), 1) < col
    zero = jnp.zeros((64, HALF), f32)
    for part in range(2):
        for block in range(4):
            rows = pl.ds(row + 64 * block, 64)
            at = slice(64 * block, 64 * block + 64)
            left = pltpu.roll(patch[part, at, 0:HALF], col, 1)
            right = pltpu.roll(patch[part, at, HALF:PW], col, 1)
            total[part, 0, rows] = total[part, 0, rows] + jnp.where(low, zero, left)
            total[part, 1, rows] = total[part, 1, rows] + jnp.where(low, left, right)
            total[part, 2, rows] = total[part, 2, rows] + jnp.where(low, right, zero)


def share_rows(total, shares, mode):
    for step in range(MODES):
        owner = lax.rem(mode + step, MODES)
        for half in range(2):
            rows = pl.ds(pl.multiple_of(PW * half + SHARE * owner, SHARE), SHARE)
            for part in range(2):
                for t in range(3):
                    shares[step][part, half, t] = total[part, t, rows].astype(bf16)


def set_rows(both, top, bottom):
    both[0:PW] = top.astype(bf16)
    both[PW:] = bottom.astype(bf16)


def set_lanes(both, stacked):
    both[:, 0:PW] = stacked[0:PW].astype(bf16)
    both[:, PW:] = stacked[PW:].astype(bf16)


def each_mode(step):
    def trip(index, _):
        for lane_set in range(UNROLL):
            step(index * UNROLL + lane_set, lane_set)
        return 0

    return lax.fori_loop(0, MODES // UNROLL, trip, 0)


def propagate_kernel(meta, own, east, south, corner, p0, p1, p2, p3, left, right, arrived, window, patch, probes, rows, lanes):
    for mode, probe in enumerate((p0, p1, p2, p3)):
        probes[mode] = probe[...]
    build_window(window, own, east, south, corner)

    def one_slot(turn, _):
        row, col, _live = corner_of(meta, turn)
        cut(window, patch, row, col)

        def one_mode(mode, lane_set):
            probe_real, probe_imag = probes[mode, 0].astype(f32), probes[mode, 1].astype(f32)
            real, imag = patch[0], patch[1]
            set_rows(rows.at[lane_set], probe_real * real - probe_imag * imag, probe_real * imag + probe_imag * real)
            set_lanes(lanes.at[lane_set], dot(left[...], rows[lane_set]))
            arrived[turn, mode] = dot(lanes[lane_set], right[...])

        return each_mode(one_mode)

    lax.fori_loop(0, 2, one_slot, 0)


def detector_kernel(meta, own, east, south, corner, arrived, measured, plus, minus, arrived_grad, g0, g1, g2, g3, window, patch, rows, lanes, far, weight, second, total):
    build_window(window, own, east, south, corner)
    total[...] = jnp.zeros_like(total)

    def one_slot(turn, _):
        row, col, live = corner_of(meta, turn)
        cut(window, patch, row, col)

        def forth(mode, lane_set):
            wave_real, wave_imag = arrived[turn, mode, :, 0:PW], arrived[turn, mode, :, PW:]
            real, imag = patch[0], patch[1]
            set_rows(rows.at[lane_set], wave_real * real - wave_imag * imag, wave_real * imag + wave_imag * real)
            set_lanes(lanes.at[lane_set], dot(plus[...], rows[lane_set]))
            field = dot(lanes[lane_set], minus[...])
            far[mode] = field
            power = field[:, 0:PW] * field[:, 0:PW] + field[:, PW:] * field[:, PW:]

            @pl.when(mode == 0)
            def _():
                weight[...] = power - measured[turn].astype(f32)

            @pl.when(mode > 0)
            def _():
                weight[...] = weight[...] + power

        each_mode(forth)
        weight[...] = jnp.where(live, weight[...], 0.0)
        second[...] = jnp.zeros_like(second)

        def back(mode, lane_set):
            scale = weight[...]
            set_rows(rows.at[lane_set], scale * far[mode, :, 0:PW], scale * far[mode, :, PW:])
            set_lanes(lanes.at[lane_set], dot(minus[...], rows[lane_set]))
            leaving = dot(lanes[lane_set], plus[...])
            grad_real, grad_imag = leaving[:, 0:PW], leaving[:, PW:]
            wave_real, wave_imag = arrived[turn, mode, :, 0:PW], arrived[turn, mode, :, PW:]
            second[0] = second[0] + (wave_real * grad_real + wave_imag * grad_imag)
            second[1] = second[1] + (wave_real * grad_imag - wave_imag * grad_real)
            real, imag = patch[0], patch[1]
            arrived_grad[turn, mode, 0:PW] = (real * grad_real + imag * grad_imag).astype(bf16)
            arrived_grad[turn, mode, PW:] = (real * grad_imag - imag * grad_real).astype(bf16)

        each_mode(back)
        place(total, second, row, col)
        return 0

    lax.fori_loop(0, 2, one_slot, 0)
    share_rows(total, (g0, g1, g2, g3), meta[2 * SLOTS + 1])


def return_kernel(meta, own, east, south, corner, arrived_grad, p0, p1, p2, p3, left, right, g0, g1, g2, g3, kept, sent, window, patch, probes, lanes, first, total, probe_total):
    for mode, probe in enumerate((p0, p1, p2, p3)):
        probes[mode] = probe[...]
    build_window(window, own, east, south, corner)
    total[...] = jnp.zeros_like(total)
    probe_total[...] = jnp.zeros_like(probe_total)

    def one_slot(turn, _):
        row, col, _live = corner_of(meta, turn)
        cut(window, patch, row, col)
        first[...] = jnp.zeros_like(first)

        def one_mode(mode, lane_set):
            set_lanes(lanes.at[lane_set], dot(left[...], arrived_grad[turn, mode]))
            grad = dot(lanes[lane_set], right[...])
            grad_real, grad_imag = grad[:, 0:PW], grad[:, PW:]
            probe_real, probe_imag = probes[mode, 0].astype(f32), probes[mode, 1].astype(f32)
            real, imag = patch[0], patch[1]
            first[0] = first[0] + (probe_real * grad_real + probe_imag * grad_imag)
            first[1] = first[1] + (probe_real * grad_imag - probe_imag * grad_real)
            probe_total[0, mode] = probe_total[0, mode] + (real * grad_real + imag * grad_imag)
            probe_total[1, mode] = probe_total[1, mode] + (real * grad_imag - imag * grad_real)

        each_mode(one_mode)
        place(total, first, row, col)
        return 0

    lax.fori_loop(0, 2, one_slot, 0)
    share_rows(total, (g0, g1, g2, g3), meta[2 * SLOTS + 1])
    core = meta[2 * SLOTS + 2]
    kept[...] = probe_total[core]
    sent[...] = probe_total[1 - core].astype(bf16)


def kernel_call(body, out_shape, scratch, name, operands, flops, limit):
    vmem = pl.BlockSpec(memory_space=pltpu.VMEM)
    smem = pl.BlockSpec(memory_space=pltpu.SMEM)
    return pl.pallas_call(
        body,
        out_shape=tuple(jax.ShapeDtypeStruct(*shape) for shape in out_shape),
        in_specs=[smem] + [vmem] * (len(operands) - 1),
        out_specs=tuple(vmem for _ in out_shape),
        scratch_shapes=[pltpu.VMEM(*shape) for shape in scratch],
        compiler_params=pltpu.CompilerParams(vmem_limit_bytes=limit << 20),
        cost_estimate=pl.CostEstimate(flops=flops, bytes_accessed=12 << 20, transcendentals=0),
        name=name,
    )(*operands)


WINDOW = ((2, 3, 2 * PW, HALF), f32)
PATCH = ((2, PW, PW), f32)
ROWS = ((UNROLL, 2 * PW, PW), bf16)
LANES = ((UNROLL, PW, 2 * PW), bf16)
PROBES = ((MODES, 2, PW, PW), bf16)
SHARES = [((2, 2, 3, SHARE, HALF), bf16)] * MODES
TRANSFORM = 8 * 16 * PW * PW * PW


def kernels(meta, pieces, all_probes, turns, matrices):
    plus, minus, left, right = matrices
    (arrived,) = kernel_call(
        propagate_kernel,
        [((2, MODES, PW, 2 * PW), f32)],
        [WINDOW, PATCH, PROBES, ROWS, LANES],
        "propagate",
        (meta, *pieces[0], *all_probes, left, right),
        TRANSFORM,
        16,
    )
    arrived_grad, *second_shares = kernel_call(
        detector_kernel,
        [((2, MODES, 2 * PW, PW), bf16)] + SHARES,
        [WINDOW, PATCH, ROWS, LANES, ((MODES, PW, 2 * PW), f32), ((PW, PW), f32), PATCH, WINDOW],
        "detector",
        (meta, *pieces[1], arrived, turns, plus, minus),
        2 * TRANSFORM,
        26,
    )
    *first_shares, kept, sent = kernel_call(
        return_kernel,
        SHARES + [((MODES, PW, PW), f32), ((MODES, PW, PW), bf16)],
        [WINDOW, PATCH, PROBES, LANES, PATCH, WINDOW, ((2, MODES, PW, PW), f32)],
        "returned",
        (meta, *pieces[0], arrived_grad, *all_probes, right, left),
        TRANSFORM,
        20,
    )
    return second_shares, first_shares, kept, sent


def toward(value, steps):
    pairs = [(t, t + steps) for t in range(TILES) if 0 <= t + steps < TILES]
    return lax.ppermute(value, "tile", pairs)


def to_mode(value, steps):
    return lax.ppermute(value, "mode", [(m, (m + steps) % MODES) for m in range(MODES)])


def tile_of(x, z, core):
    return (x * 8 + z) * 2 + core


def to_core(value):
    return lax.ppermute(value, "tile", [(t, t ^ 1) for t in range(TILES)])


def send_rows(shares):
    return [shares[0]] + [to_mode(shares[step], step) for step in range(1, MODES)]


def add_up(values):
    total = values[0].astype(f32)
    for value in values[1:]:
        total = total + value.astype(f32)
    return total


def exchange(value):
    groups = [[tile_of(x, z, c) for x in range(4) for z in range(8)] for c in range(2)]
    return lax.all_to_all(value, "tile", 0, 0, axis_index_groups=groups)


def shards(object_tiles, probes, measured, offsets, counts):
    matrices = block_forms(*lax.optimization_barrier(tuple(jnp.asarray(table) for table in constants())))
    tile = lax.axis_index("tile")
    mode = lax.axis_index("mode")
    core = lax.rem(tile, 2)
    meta = jnp.concatenate([offsets.reshape(-1), counts, jnp.stack([mode, core])]).astype(jnp.int32)
    pieces = []
    for depth in range(2):
        own = object_tiles[0, depth]
        pieces.append((own, toward(own, -1), toward(own[:, :, HALF:], -TGX), toward(own, -TGX - 1)))
        if depth == 0:
            probe = probes[0].astype(bf16)
            all_probes = [probe] + [to_mode(probe, MODES - step) for step in range(1, MODES)]
    turns = lax.dynamic_index_in_dim(measured[0].reshape(2, MODES, PW, PW), mode, 1, keepdims=False)

    second_shares, first_shares, kept, sent = kernels(meta, pieces, all_probes, turns, matrices)
    with jax.named_scope("core_out"):
        halves = kept + to_core(sent).astype(f32)
    with jax.named_scope("probe_rows"):
        mine = add_up(send_rows([halves[0]] + [halves[step].astype(bf16) for step in range(1, MODES)]))
    with jax.named_scope("gather_sum"):
        parts = exchange(mine.astype(bf16).reshape(32, 8, PW))
        part = jnp.sum(parts.astype(f32), axis=0).astype(bf16)
    with jax.named_scope("second_rows"):
        second = add_up(send_rows(second_shares))
    with jax.named_scope("first_rows"):
        first = add_up(send_rows(first_shares))
    rows = jnp.stack([first, second])
    with jax.named_scope("eastward"):
        eastward = toward(rows[:, :, :, 1:].astype(bf16), 1).astype(f32)
    joined = jnp.concatenate([eastward[:, :, :, 0], eastward[:, :, :, 1] + rows[:, :, :, 0]], axis=-1)
    with jax.named_scope("southward"):
        object_grad = joined[:, :, 0] + toward(joined[:, :, 1].astype(bf16), TGX).astype(f32)
    with jax.named_scope("spread"):
        plane = exchange(jnp.broadcast_to(part[None], (32, 8, PW))).reshape(PW, PW)
    with jax.named_scope("core_back"):
        other = to_core(plane)
    real = jnp.where(core == 0, plane, other)
    imag = jnp.where(core == 0, other, plane)
    return (object_grad[None], jnp.stack([real, imag]).astype(f32)[None])


def solution(mesh):
    placed = (
        P("tile", None, None, None, None),
        P("mode", None, None, None),
        P("tile", None, None, None),
        P("tile", None, None),
        P("tile"),
    )
    return jax.shard_map(
        shards,
        mesh=mesh,
        in_specs=placed,
        out_specs=(P("tile", None, None, "mode", None), P("mode", None, None, None)),
        check_vma=False,
    )
```

```python
import math

import jax
import jax.numpy as jnp
import numpy as np
from jax import lax
from jax.experimental import pallas as pl
from jax.experimental.pallas import tpu as pltpu
from jax.sharding import PartitionSpec as P


PW = 256
HALF = 128
SLOTS = 8
MODES = 4
TGX = 8
TILES = 64
SHARE = PW // MODES
UNROLL = 4
f32 = jnp.float32
bf16 = jnp.bfloat16


def constants():
    indices = np.arange(PW)
    angles = ((indices[:, None] * indices[None, :]) % PW) * (2.0 * math.pi / PW)
    cosine = (np.cos(angles) / math.sqrt(PW)).astype(bf16)
    sine = (np.sin(angles) / math.sqrt(PW)).astype(bf16)
    frequency = (((indices + PW // 2) % PW) - PW // 2) / PW
    phase = np.exp(-1j * math.pi * (PW / 8.0) * frequency * frequency)
    table = cosine.astype(np.float64) - 1j * sine.astype(np.float64)
    hop = np.conj(table) @ (phase[:, None] * table)
    hop_real = hop.real.astype(bf16)
    hop_imag = hop.imag.astype(bf16)
    return cosine, sine, hop_real, hop_imag


def block_forms(cosine, sine, hop_real, hop_imag):
    return (
        jnp.block([[cosine, sine], [-sine, cosine]]),
        jnp.block([[cosine, -sine], [sine, cosine]]),
        jnp.block([[hop_real, -hop_imag], [hop_imag, hop_real]]),
        jnp.block([[hop_real, hop_imag], [-hop_imag, hop_real]]),
    )


def dot(left, right):
    return jnp.dot(left, right, preferred_element_type=f32)


def build_window(window, depth, meta, own, east, lower):
    for part in range(2):
        window[part, 0, 0:PW] = own[depth, part, :, HALF:].astype(f32)
        for lane_tile in range(2):
            lanes = slice(HALF * lane_tile, HALF * lane_tile + HALF)
            window[part, 1 + lane_tile, 0:PW] = east[depth, part, :, lanes].astype(f32)
        for step in range(MODES):
            owner = lax.rem(meta[2 * SLOTS + 1] + step, MODES)
            rows = pl.ds(pl.multiple_of(PW + SHARE * owner, SHARE), SHARE)
            for t in range(3):
                window[part, t, rows] = lower[step][depth, part, :, HALF * t : HALF * t + HALF].astype(f32)


def load_probes(probes, meta, own, near, far):
    core = meta[2 * SLOTS + 2]
    probes[0] = own[...]
    for step in range(1, MODES):
        probes[step, core] = near[step - 1]
        probes[step, 1 - core] = far[step - 1]


def corner_of(meta, turn):
    slot = meta[2 * SLOTS + 1] + MODES * turn
    return meta[2 * slot], meta[2 * slot + 1] - HALF, slot < meta[2 * SLOTS]


def cut(window, patch, row, col):
    keep = lax.broadcasted_iota(jnp.int32, (64, HALF), 1) < HALF - col
    turn = jnp.where(col == 0, 0, HALF - col)
    for part in range(2):
        for block in range(4):
            rows = pl.ds(row + 64 * block, 64)
            rolled = [pltpu.roll(window[part, t, rows], turn, 1) for t in range(3)]
            at = slice(64 * block, 64 * block + 64)
            patch[part, at, 0:HALF] = jnp.where(keep, rolled[0], rolled[1])
            patch[part, at, HALF:PW] = jnp.where(keep, rolled[1], rolled[2])


def place(total, patch, row, col):
    low = lax.broadcasted_iota(jnp.int32, (64, HALF), 1) < col
    zero = jnp.zeros((64, HALF), f32)
    for part in range(2):
        for block in range(4):
            rows = pl.ds(row + 64 * block, 64)
            at = slice(64 * block, 64 * block + 64)
            left = pltpu.roll(patch[part, at, 0:HALF], col, 1)
            right = pltpu.roll(patch[part, at, HALF:PW], col, 1)
            total[part, 0, rows] = total[part, 0, rows] + jnp.where(low, zero, left)
            total[part, 1, rows] = total[part, 1, rows] + jnp.where(low, left, right)
            total[part, 2, rows] = total[part, 2, rows] + jnp.where(low, right, zero)


def share_rows(total, shares, mode):
    for step in range(MODES):
        owner = lax.rem(mode + step, MODES)
        for half in range(2):
            rows = pl.ds(pl.multiple_of(PW * half + SHARE * owner, SHARE), SHARE)
            for part in range(2):
                for t in range(3):
                    shares[step][part, half, t] = total[part, t, rows].astype(bf16)


def set_rows(both, top, bottom):
    both[0:PW] = top.astype(bf16)
    both[PW:] = bottom.astype(bf16)


def set_lanes(both, stacked):
    both[:, 0:PW] = stacked[0:PW].astype(bf16)
    both[:, PW:] = stacked[PW:].astype(bf16)


def each_mode(step):
    def trip(index, _):
        for lane_set in range(UNROLL):
            step(index * UNROLL + lane_set, lane_set)
        return 0

    return lax.fori_loop(0, MODES // UNROLL, trip, 0)


def propagate_kernel(meta, own, east, l0, l1, l2, l3, probe, near, far, left, right, arrived, window, patch, probes, rows, lanes):
    load_probes(probes, meta, probe, near, far)
    build_window(window, 0, meta, own, east, (l0, l1, l2, l3))

    def one_slot(turn, _):
        row, col, _ = corner_of(meta, turn)
        cut(window, patch, row, col)

        def one_mode(mode, lane_set):
            probe_real, probe_imag = probes[mode, 0].astype(f32), probes[mode, 1].astype(f32)
            real, imag = patch[0], patch[1]
            set_rows(rows.at[lane_set], probe_real * real - probe_imag * imag, probe_real * imag + probe_imag * real)
            set_lanes(lanes.at[lane_set], dot(left[...], rows[lane_set]))
            arrived[turn, mode] = dot(lanes[lane_set], right[...])

        return each_mode(one_mode)

    lax.fori_loop(0, 2, one_slot, 0)


def detector_kernel(meta, own, east, l0, l1, l2, l3, arrived, measured, plus, minus, arrived_grad, g0, g1, g2, g3, window, patch, rows, lanes, far, weight, second, total):
    build_window(window, 1, meta, own, east, (l0, l1, l2, l3))
    total[...] = jnp.zeros_like(total)

    def one_slot(turn, _):
        row, col, live = corner_of(meta, turn)
        cut(window, patch, row, col)

        def forth(mode, lane_set):
            wave_real, wave_imag = arrived[turn, mode, :, 0:PW], arrived[turn, mode, :, PW:]
            real, imag = patch[0], patch[1]
            set_rows(rows.at[lane_set], wave_real * real - wave_imag * imag, wave_real * imag + wave_imag * real)
            set_lanes(lanes.at[lane_set], dot(plus[...], rows[lane_set]))
            field = dot(lanes[lane_set], minus[...])
            far[mode] = field
            power = field[:, 0:PW] * field[:, 0:PW] + field[:, PW:] * field[:, PW:]

            @pl.when(mode == 0)
            def _():
                weight[...] = power - measured[turn].astype(f32)

            @pl.when(mode > 0)
            def _():
                weight[...] = weight[...] + power

        each_mode(forth)
        weight[...] = jnp.where(live, weight[...], 0.0)
        second[...] = jnp.zeros_like(second)

        def back(mode, lane_set):
            scale = weight[...]
            set_rows(rows.at[lane_set], scale * far[mode, :, 0:PW], scale * far[mode, :, PW:])
            set_lanes(lanes.at[lane_set], dot(minus[...], rows[lane_set]))
            leaving = dot(lanes[lane_set], plus[...])
            grad_real, grad_imag = leaving[:, 0:PW], leaving[:, PW:]
            wave_real, wave_imag = arrived[turn, mode, :, 0:PW], arrived[turn, mode, :, PW:]
            second[0] = second[0] + (wave_real * grad_real + wave_imag * grad_imag)
            second[1] = second[1] + (wave_real * grad_imag - wave_imag * grad_real)
            real, imag = patch[0], patch[1]
            arrived_grad[turn, mode, 0:PW] = (real * grad_real + imag * grad_imag).astype(bf16)
            arrived_grad[turn, mode, PW:] = (real * grad_imag - imag * grad_real).astype(bf16)

        each_mode(back)
        place(total, second, row, col)
        return 0

    lax.fori_loop(0, 2, one_slot, 0)
    share_rows(total, (g0, g1, g2, g3), meta[2 * SLOTS + 1])


def return_kernel(meta, own, east, l0, l1, l2, l3, arrived_grad, probe, near, far, left, right, g0, g1, g2, g3, kept, sent, window, patch, probes, lanes, first, total, probe_total):
    load_probes(probes, meta, probe, near, far)
    build_window(window, 0, meta, own, east, (l0, l1, l2, l3))
    total[...] = jnp.zeros_like(total)
    probe_total[...] = jnp.zeros_like(probe_total)

    def one_slot(turn, _):
        row, col, _ = corner_of(meta, turn)
        cut(window, patch, row, col)
        first[...] = jnp.zeros_like(first)

        def one_mode(mode, lane_set):
            set_lanes(lanes.at[lane_set], dot(left[...], arrived_grad[turn, mode]))
            grad = dot(lanes[lane_set], right[...])
            grad_real, grad_imag = grad[:, 0:PW], grad[:, PW:]
            probe_real, probe_imag = probes[mode, 0].astype(f32), probes[mode, 1].astype(f32)
            real, imag = patch[0], patch[1]
            first[0] = first[0] + (probe_real * grad_real + probe_imag * grad_imag)
            first[1] = first[1] + (probe_real * grad_imag - probe_imag * grad_real)
            probe_total[0, mode] = probe_total[0, mode] + (real * grad_real + imag * grad_imag)
            probe_total[1, mode] = probe_total[1, mode] + (real * grad_imag - imag * grad_real)

        each_mode(one_mode)
        place(total, first, row, col)
        return 0

    lax.fori_loop(0, 2, one_slot, 0)
    share_rows(total, (g0, g1, g2, g3), meta[2 * SLOTS + 1])
    core = meta[2 * SLOTS + 2]
    kept[...] = probe_total[core]
    sent[...] = probe_total[1 - core].astype(bf16)


def kernel_call(body, out_shape, scratch, operands, flops, limit):
    vmem = pl.BlockSpec(memory_space=pltpu.VMEM)
    smem = pl.BlockSpec(memory_space=pltpu.SMEM)
    return pl.pallas_call(
        body,
        out_shape=tuple(jax.ShapeDtypeStruct(*shape) for shape in out_shape),
        in_specs=[smem] + [vmem] * (len(operands) - 1),
        out_specs=tuple(vmem for _ in out_shape),
        scratch_shapes=[pltpu.VMEM(*shape) for shape in scratch],
        compiler_params=pltpu.CompilerParams(vmem_limit_bytes=limit << 20),
        cost_estimate=pl.CostEstimate(flops=flops, bytes_accessed=12 << 20, transcendentals=0),
    )(*operands)


WINDOW = ((2, 3, 2 * PW, HALF), f32)
PATCH = ((2, PW, PW), f32)
ROWS = ((UNROLL, 2 * PW, PW), bf16)
LANES = ((UNROLL, PW, 2 * PW), bf16)
PROBES = ((MODES, 2, PW, PW), bf16)
SHARES = [((2, 2, 3, SHARE, HALF), bf16)] * MODES
TRANSFORM = 8 * 16 * PW * PW * PW


def kernels(meta, pieces, all_probes, turns, matrices):
    plus, minus, left, right = matrices
    (arrived,) = kernel_call(
        propagate_kernel,
        [((2, MODES, PW, 2 * PW), f32)],
        [WINDOW, PATCH, PROBES, ROWS, LANES],
        (meta, *pieces, *all_probes, left, right),
        TRANSFORM,
        16,
    )
    arrived_grad, *second_shares = kernel_call(
        detector_kernel,
        [((2, MODES, 2 * PW, PW), bf16)] + SHARES,
        [WINDOW, PATCH, ROWS, LANES, ((MODES, PW, 2 * PW), f32), ((PW, PW), f32), PATCH, WINDOW],
        (meta, *pieces, arrived, turns, plus, minus),
        2 * TRANSFORM,
        26,
    )
    *first_shares, kept, sent = kernel_call(
        return_kernel,
        SHARES + [((MODES, PW, PW), f32), ((MODES, PW, PW), bf16)],
        [WINDOW, PATCH, PROBES, LANES, PATCH, WINDOW, ((2, MODES, PW, PW), f32)],
        (meta, *pieces, arrived_grad, *all_probes, right, left),
        TRANSFORM,
        20,
    )
    return second_shares, first_shares, kept, sent


def toward(value, steps):
    pairs = [(t, t + steps) for t in range(TILES) if 0 <= t + steps < TILES]
    return lax.ppermute(value, "tile", pairs)


def to_mode(value, steps):
    return lax.ppermute(value, "mode", [(m, (m + steps) % MODES) for m in range(MODES)])


def tile_of(x, z, core):
    return (x * 8 + z) * 2 + core


def to_core(value):
    return lax.ppermute(value, "tile", [(t, t ^ 1) for t in range(TILES)])


def send_rows(shares):
    received = [shares[0]]
    for step in range(1, MODES):
        received.append(to_mode(shares[step], step))
    return received


def fetch(value):
    received = []
    for step in range(1, MODES):
        received.append(to_mode(value, MODES - step))
    return received


def add_up(values):
    total = values[0].astype(f32)
    for value in values[1:]:
        total = total + value.astype(f32)
    return total


def exchange(value):
    groups = [[tile_of(x, z, c) for x in range(4) for z in range(8)] for c in range(2)]
    return lax.all_to_all(value, "tile", 0, 0, axis_index_groups=groups)


def one_step(object_tiles, probes, measured, offsets, counts):
    tile = lax.axis_index("tile")
    mode = lax.axis_index("mode")
    core = lax.rem(tile, 2)
    own = object_tiles[0]
    quarter = lax.dynamic_slice_in_dim(own, SHARE * mode, SHARE, 2)
    corner = toward(quarter, -TGX - 1)
    south = toward(quarter[..., HALF:], -TGX)
    probe = probes[0].astype(bf16)
    near = jnp.stack(fetch(lax.dynamic_index_in_dim(probe, core, 0, keepdims=False)))
    far = to_core(near)
    east = toward(own, -1)
    lower = jnp.concatenate([south, corner], axis=-1)
    quarters = [lower] + fetch(lower)
    pieces = (own, east, *quarters)
    all_probes = (probe, near, far)
    matrices = block_forms(*lax.optimization_barrier(tuple(jnp.asarray(table) for table in constants())))
    meta = jnp.concatenate([offsets.reshape(-1), counts, jnp.stack([mode, core])]).astype(jnp.int32)
    turns = lax.dynamic_index_in_dim(measured[0].reshape(2, MODES, PW, PW), mode, 1, keepdims=False)
    second_shares, first_shares, kept, sent = kernels(meta, pieces, all_probes, turns, matrices)
    second = add_up(send_rows(second_shares))
    halves = kept + to_core(sent).astype(f32)
    mine = add_up(send_rows([halves[0]] + [halves[step].astype(bf16) for step in range(1, MODES)]))
    parts = exchange(mine.astype(bf16).reshape(32, 8, PW))
    part = jnp.sum(parts.astype(f32), axis=0).astype(bf16)
    first = add_up(send_rows(first_shares))
    rows = jnp.stack([first, second])
    eastward = toward(rows[:, :, :, 1:].astype(bf16), 1).astype(f32)
    joined = jnp.concatenate([eastward[:, :, :, 0], eastward[:, :, :, 1] + rows[:, :, :, 0]], axis=-1)
    object_grad = joined[:, :, 0] + toward(joined[:, :, 1].astype(bf16), TGX).astype(f32)
    plane = exchange(jnp.broadcast_to(part[None], (32, 8, PW))).reshape(PW, PW)
    other = to_core(plane)
    real = jnp.where(core == 0, plane, other)
    imag = jnp.where(core == 0, other, plane)
    return (object_grad[None], jnp.stack([real, imag]).astype(f32)[None])


def solution(mesh):
    placed = (
        P("tile", None, None, None, None),
        P("mode", None, None, None),
        P("tile", None, None, None),
        P("tile", None, None),
        P("tile"),
    )
    return jax.shard_map(
        one_step,
        mesh=mesh,
        in_specs=placed,
        out_specs=(P("tile", None, None, "mode", None), P("mode", None, None, None)),
        check_vma=False,
    )
```

```python
import math

import jax
import jax.numpy as jnp
import numpy as np
from jax import lax
from jax.experimental import pallas as pl
from jax.experimental.pallas import tpu as pltpu
from jax.sharding import PartitionSpec as P


PW = 256
HALF = 128
SLOTS = 8
MODES = 4
TGX = 8
TILES = 64
SHARE = PW // MODES
UNROLL = 4
f32 = jnp.float32
bf16 = jnp.bfloat16


def constants():
    indices = np.arange(PW)
    angles = ((indices[:, None] * indices[None, :]) % PW) * (2.0 * math.pi / PW)
    cosine = (np.cos(angles) / math.sqrt(PW)).astype(bf16)
    sine = (np.sin(angles) / math.sqrt(PW)).astype(bf16)
    frequency = (((indices + PW // 2) % PW) - PW // 2) / PW
    phase = np.exp(-1j * math.pi * (PW / 8.0) * frequency * frequency)
    table = cosine.astype(np.float64) - 1j * sine.astype(np.float64)
    hop = np.conj(table) @ (phase[:, None] * table)
    hop_real = hop.real.astype(bf16)
    hop_imag = hop.imag.astype(bf16)
    return cosine, sine, hop_real, hop_imag


def block_forms(cosine, sine, hop_real, hop_imag):
    return (
        jnp.block([[cosine, sine], [-sine, cosine]]),
        jnp.block([[cosine, -sine], [sine, cosine]]),
        jnp.block([[hop_real, -hop_imag], [hop_imag, hop_real]]),
        jnp.block([[hop_real, hop_imag], [-hop_imag, hop_real]]),
    )


def dot(left, right):
    return jnp.dot(left, right, preferred_element_type=f32)


def build_window(window, depth, meta, own, east, lower):
    for part in range(2):
        window[part, 0, 0:PW] = own[depth, part, :, HALF:].astype(f32)
        for lane_tile in range(2):
            lanes = slice(HALF * lane_tile, HALF * lane_tile + HALF)
            window[part, 1 + lane_tile, 0:PW] = east[depth, part, :, lanes].astype(f32)
        for step in range(MODES):
            owner = lax.rem(meta[2 * SLOTS + 1] + step, MODES)
            rows = pl.ds(pl.multiple_of(PW + SHARE * owner, SHARE), SHARE)
            for t in range(3):
                window[part, t, rows] = lower[step][depth, part, :, HALF * t : HALF * t + HALF].astype(f32)


def load_probes(probes, meta, own, near, far):
    core = meta[2 * SLOTS + 2]
    probes[0] = own[...]
    for step in range(1, MODES):
        probes[step, core] = near[step - 1]
        probes[step, 1 - core] = far[step - 1]


def corner_of(meta, turn):
    slot = meta[2 * SLOTS + 1] + MODES * turn
    return meta[2 * slot], meta[2 * slot + 1] - HALF, slot < meta[2 * SLOTS]


def cut(window, patch, row, col):
    keep = lax.broadcasted_iota(jnp.int32, (64, HALF), 1) < HALF - col
    turn = jnp.where(col == 0, 0, HALF - col)
    for part in range(2):
        for block in range(4):
            rows = pl.ds(row + 64 * block, 64)
            rolled = [pltpu.roll(window[part, t, rows], turn, 1) for t in range(3)]
            at = slice(64 * block, 64 * block + 64)
            patch[part, at, 0:HALF] = jnp.where(keep, rolled[0], rolled[1])
            patch[part, at, HALF:PW] = jnp.where(keep, rolled[1], rolled[2])


def place(total, patch, row, col):
    low = lax.broadcasted_iota(jnp.int32, (64, HALF), 1) < col
    zero = jnp.zeros((64, HALF), f32)
    for part in range(2):
        for block in range(4):
            rows = pl.ds(row + 64 * block, 64)
            at = slice(64 * block, 64 * block + 64)
            left = pltpu.roll(patch[part, at, 0:HALF], col, 1)
            right = pltpu.roll(patch[part, at, HALF:PW], col, 1)
            total[part, 0, rows] = total[part, 0, rows] + jnp.where(low, zero, left)
            total[part, 1, rows] = total[part, 1, rows] + jnp.where(low, left, right)
            total[part, 2, rows] = total[part, 2, rows] + jnp.where(low, right, zero)


def share_rows(totals, shares, mode):
    for step in range(MODES):
        owner = lax.rem(mode + step, MODES)
        for half in range(2):
            rows = pl.ds(pl.multiple_of(PW * half + SHARE * owner, SHARE), SHARE)
            for part in range(2):
                for t in range(3):
                    for depth in range(2):
                        shares[step][depth, part, half, t] = totals[depth][part, t, rows].astype(bf16)


def set_rows(both, top, bottom):
    both[0:PW] = top.astype(bf16)
    both[PW:] = bottom.astype(bf16)


def set_lanes(both, stacked):
    both[:, 0:PW] = stacked[0:PW].astype(bf16)
    both[:, PW:] = stacked[PW:].astype(bf16)


def each_mode(step):
    def trip(index, _):
        for lane_set in range(UNROLL):
            step(index * UNROLL + lane_set, lane_set)
        return 0

    return lax.fori_loop(0, MODES // UNROLL, trip, 0)


def propagate_kernel(meta, own, east, l0, l1, l2, l3, probe, near, far, left, right, arrived, patches, window, probes, rows, lanes):
    load_probes(probes, meta, probe, near, far)
    build_window(window, 0, meta, own, east, (l0, l1, l2, l3))

    def one_slot(turn, _):
        row, col, _ = corner_of(meta, turn)
        patch = patches.at[turn]
        cut(window, patch, row, col)

        def one_mode(mode, lane_set):
            probe_real, probe_imag = probes[mode, 0].astype(f32), probes[mode, 1].astype(f32)
            real, imag = patch[0], patch[1]
            set_rows(rows.at[lane_set], probe_real * real - probe_imag * imag, probe_real * imag + probe_imag * real)
            set_lanes(lanes.at[lane_set], dot(left[...], rows[lane_set]))
            arrived[turn, mode] = dot(lanes[lane_set], right[...])

        return each_mode(one_mode)

    lax.fori_loop(0, 2, one_slot, 0)


def detector_kernel(meta, own, east, l0, l1, l2, l3, arrived, measured, plus, minus, arrived_grad, total, window, patch, rows, lanes, far, weight, second):
    build_window(window, 1, meta, own, east, (l0, l1, l2, l3))
    total[...] = jnp.zeros_like(total)

    def one_slot(turn, _):
        row, col, live = corner_of(meta, turn)
        cut(window, patch, row, col)

        def forth(mode, lane_set):
            wave_real, wave_imag = arrived[turn, mode, :, 0:PW], arrived[turn, mode, :, PW:]
            real, imag = patch[0], patch[1]
            set_rows(rows.at[lane_set], wave_real * real - wave_imag * imag, wave_real * imag + wave_imag * real)
            set_lanes(lanes.at[lane_set], dot(plus[...], rows[lane_set]))
            field = dot(lanes[lane_set], minus[...])
            far[mode] = field
            power = field[:, 0:PW] * field[:, 0:PW] + field[:, PW:] * field[:, PW:]

            @pl.when(mode == 0)
            def _():
                weight[...] = power - measured[turn].astype(f32)

            @pl.when(mode > 0)
            def _():
                weight[...] = weight[...] + power

        each_mode(forth)
        weight[...] = jnp.where(live, weight[...], 0.0)
        second[...] = jnp.zeros_like(second)

        def back(mode, lane_set):
            scale = weight[...]
            set_rows(rows.at[lane_set], scale * far[mode, :, 0:PW], scale * far[mode, :, PW:])
            set_lanes(lanes.at[lane_set], dot(minus[...], rows[lane_set]))
            leaving = dot(lanes[lane_set], plus[...])
            grad_real, grad_imag = leaving[:, 0:PW], leaving[:, PW:]
            wave_real, wave_imag = arrived[turn, mode, :, 0:PW], arrived[turn, mode, :, PW:]
            second[0] = second[0] + (wave_real * grad_real + wave_imag * grad_imag)
            second[1] = second[1] + (wave_real * grad_imag - wave_imag * grad_real)
            real, imag = patch[0], patch[1]
            arrived_grad[turn, mode, 0:PW] = (real * grad_real + imag * grad_imag).astype(bf16)
            arrived_grad[turn, mode, PW:] = (real * grad_imag - imag * grad_real).astype(bf16)

        each_mode(back)
        place(total, second, row, col)
        return 0

    lax.fori_loop(0, 2, one_slot, 0)


def return_kernel(meta, patches, arrived_grad, second_total, probe, near, far, left, right, g0, g1, g2, g3, kept, sent, probes, lanes, first, total, probe_total):
    load_probes(probes, meta, probe, near, far)
    total[...] = jnp.zeros_like(total)
    probe_total[...] = jnp.zeros_like(probe_total)

    def one_slot(turn, _):
        row, col, _ = corner_of(meta, turn)
        patch = patches.at[turn]
        first[...] = jnp.zeros_like(first)

        def one_mode(mode, lane_set):
            set_lanes(lanes.at[lane_set], dot(left[...], arrived_grad[turn, mode]))
            grad = dot(lanes[lane_set], right[...])
            grad_real, grad_imag = grad[:, 0:PW], grad[:, PW:]
            probe_real, probe_imag = probes[mode, 0].astype(f32), probes[mode, 1].astype(f32)
            real, imag = patch[0], patch[1]
            first[0] = first[0] + (probe_real * grad_real + probe_imag * grad_imag)
            first[1] = first[1] + (probe_real * grad_imag - probe_imag * grad_real)
            probe_total[0, mode] = probe_total[0, mode] + (real * grad_real + imag * grad_imag)
            probe_total[1, mode] = probe_total[1, mode] + (real * grad_imag - imag * grad_real)

        each_mode(one_mode)
        place(total, first, row, col)
        return 0

    lax.fori_loop(0, 2, one_slot, 0)
    share_rows((total, second_total), (g0, g1, g2, g3), meta[2 * SLOTS + 1])
    core = meta[2 * SLOTS + 2]
    kept[...] = probe_total[core]
    sent[...] = probe_total[1 - core].astype(bf16)


def kernel_call(body, out_shape, scratch, operands, flops, limit):
    vmem = pl.BlockSpec(memory_space=pltpu.VMEM)
    smem = pl.BlockSpec(memory_space=pltpu.SMEM)
    return pl.pallas_call(
        body,
        out_shape=tuple(jax.ShapeDtypeStruct(*shape) for shape in out_shape),
        in_specs=[smem] + [vmem] * (len(operands) - 1),
        out_specs=tuple(vmem for _ in out_shape),
        scratch_shapes=[pltpu.VMEM(*shape) for shape in scratch],
        compiler_params=pltpu.CompilerParams(vmem_limit_bytes=limit << 20),
        cost_estimate=pl.CostEstimate(flops=flops, bytes_accessed=12 << 20, transcendentals=0),
    )(*operands)


WINDOW = ((2, 3, 2 * PW, HALF), f32)
PATCH = ((2, PW, PW), f32)
ROWS = ((UNROLL, 2 * PW, PW), bf16)
LANES = ((UNROLL, PW, 2 * PW), bf16)
PROBES = ((MODES, 2, PW, PW), bf16)
SHARES = [((2, 2, 2, 3, SHARE, HALF), bf16)] * MODES
TRANSFORM = 8 * 16 * PW * PW * PW


def kernels(meta, pieces, all_probes, turns, matrices):
    plus, minus, left, right = matrices
    arrived, patches = kernel_call(
        propagate_kernel,
        [((2, MODES, PW, 2 * PW), f32), ((2, 2, PW, PW), f32)],
        [WINDOW, PROBES, ROWS, LANES],
        (meta, *pieces, *all_probes, left, right),
        TRANSFORM,
        16,
    )
    arrived_grad, second_total = kernel_call(
        detector_kernel,
        [((2, MODES, 2 * PW, PW), bf16), WINDOW],
        [WINDOW, PATCH, ROWS, LANES, ((MODES, PW, 2 * PW), f32), ((PW, PW), f32), PATCH],
        (meta, *pieces, arrived, turns, plus, minus),
        2 * TRANSFORM,
        26,
    )
    *shares, kept, sent = kernel_call(
        return_kernel,
        SHARES + [((MODES, PW, PW), f32), ((MODES, PW, PW), bf16)],
        [PROBES, LANES, PATCH, WINDOW, ((2, MODES, PW, PW), f32)],
        (meta, patches, arrived_grad, second_total, *all_probes, right, left),
        TRANSFORM,
        20,
    )
    return shares, kept, sent


def toward(value, steps):
    pairs = [(t, t + steps) for t in range(TILES) if 0 <= t + steps < TILES]
    return lax.ppermute(value, "tile", pairs)


def to_mode(value, steps):
    return lax.ppermute(value, "mode", [(m, (m + steps) % MODES) for m in range(MODES)])


def tile_of(x, z, core):
    return (x * 8 + z) * 2 + core


def to_core(value):
    return lax.ppermute(value, "tile", [(t, t ^ 1) for t in range(TILES)])


def send_rows(shares):
    received = [shares[0]]
    for step in range(1, MODES):
        received.append(to_mode(shares[step], step))
    return received


def fetch(value):
    received = []
    for step in range(1, MODES):
        received.append(to_mode(value, MODES - step))
    return received


def add_up(values):
    total = values[0].astype(f32)
    for value in values[1:]:
        total = total + value.astype(f32)
    return total


def exchange(value):
    groups = [[tile_of(x, z, c) for x in range(4) for z in range(8)] for c in range(2)]
    return lax.all_to_all(value, "tile", 0, 0, axis_index_groups=groups)


def one_step(object_tiles, probes, measured, offsets, counts):
    tile = lax.axis_index("tile")
    mode = lax.axis_index("mode")
    core = lax.rem(tile, 2)
    own = object_tiles[0]
    quarter = lax.dynamic_slice_in_dim(own, SHARE * mode, SHARE, 2)
    corner = toward(quarter, -TGX - 1)
    south = toward(quarter[..., HALF:], -TGX)
    near = fetch(lax.dynamic_index_in_dim(probes[0], core, 0, keepdims=False).astype(bf16))
    near = jnp.stack(near)
    far = to_core(near)
    east = toward(own, -1)
    lower = jnp.concatenate([south, corner], axis=-1)
    quarters = [lower] + fetch(lower)
    pieces = (own, east, *quarters)
    probe = probes[0].astype(bf16)
    all_probes = (probe, near, far)
    matrices = block_forms(*lax.optimization_barrier(tuple(jnp.asarray(table) for table in constants())))
    meta = jnp.concatenate([offsets.reshape(-1), counts, jnp.stack([mode, core])]).astype(jnp.int32)
    turns = lax.dynamic_index_in_dim(measured[0].reshape(2, MODES, PW, PW), mode, 1, keepdims=False)
    shares, kept, sent = kernels(meta, pieces, all_probes, turns, matrices)
    halves = kept + to_core(sent).astype(f32)
    mine = add_up(send_rows([halves[0]] + [halves[step].astype(bf16) for step in range(1, MODES)]))
    parts = exchange(mine.astype(bf16).reshape(32, 8, PW))
    part = jnp.sum(parts.astype(f32), axis=0).astype(bf16)
    rows = add_up(send_rows(shares))
    eastward = toward(rows[:, :, :, 1:].astype(bf16), 1).astype(f32)
    joined = jnp.concatenate([eastward[:, :, :, 0], eastward[:, :, :, 1] + rows[:, :, :, 0]], axis=-1)
    object_grad = joined[:, :, 0] + toward(joined[:, :, 1].astype(bf16), TGX).astype(f32)
    plane = exchange(jnp.broadcast_to(part[None], (32, 8, PW))).reshape(PW, PW)
    other = to_core(plane)
    mine_first = (jnp.arange(2, dtype=jnp.int32) == core)[:, None, None]
    probe_grad = jnp.where(mine_first, plane[None].astype(f32), other[None].astype(f32))
    return (object_grad[None], probe_grad[None])


def solution(mesh):
    placed = (
        P("tile", None, None, None, None),
        P("mode", None, None, None),
        P("tile", None, None, None),
        P("tile", None, None),
        P("tile"),
    )
    return jax.shard_map(
        one_step,
        mesh=mesh,
        in_specs=placed,
        out_specs=(P("tile", None, None, "mode", None), P("mode", None, None, None)),
        check_vma=False,
    )
```

```python
import math

import jax
import jax.numpy as jnp
import numpy as np
from jax import lax
from jax.experimental import pallas as pl
from jax.experimental.pallas import tpu as pltpu
from jax.sharding import PartitionSpec as P


PW = 256
HALF = 128
SLOTS = 8
MODES = 4
TGX = 8
TILES = 64
SHARE = PW // MODES
UNROLL = 4
f32 = jnp.float32
bf16 = jnp.bfloat16


def constants():
    indices = np.arange(PW)
    angles = ((indices[:, None] * indices[None, :]) % PW) * (2.0 * math.pi / PW)
    cosine = (np.cos(angles) / math.sqrt(PW)).astype(bf16)
    sine = (np.sin(angles) / math.sqrt(PW)).astype(bf16)
    frequency = (((indices + PW // 2) % PW) - PW // 2) / PW
    phase = np.exp(-1j * math.pi * (PW / 8.0) * frequency * frequency)
    table = cosine.astype(np.float64) - 1j * sine.astype(np.float64)
    hop = np.conj(table) @ (phase[:, None] * table)
    hop_real = hop.real.astype(bf16)
    hop_imag = hop.imag.astype(bf16)
    return cosine, sine, -sine, hop_real, hop_imag, -hop_imag


def block_forms(cosine, sine, minus_sine, hop_real, hop_imag, minus_imag):
    return (
        jnp.block([[cosine, sine], [minus_sine, cosine]]),
        jnp.block([[cosine, minus_sine], [sine, cosine]]),
        jnp.block([[hop_real, minus_imag], [hop_imag, hop_real]]),
        jnp.block([[hop_real, hop_imag], [minus_imag, hop_real]]),
    )


def dot(left, right):
    return jnp.dot(left, right, preferred_element_type=f32)


def build_window(window, depth, meta, own, east, lower):
    for part in range(2):
        window[part, 0, 0:PW] = own[depth, part, :, HALF:].astype(f32)
        for lane_tile in range(2):
            lanes = slice(HALF * lane_tile, HALF * lane_tile + HALF)
            window[part, 1 + lane_tile, 0:PW] = east[depth, part, :, lanes].astype(f32)
        for step in range(MODES):
            owner = lax.rem(meta[2 * SLOTS + 1] + step, MODES)
            rows = pl.ds(pl.multiple_of(PW + SHARE * owner, SHARE), SHARE)
            for t in range(3):
                window[part, t, rows] = lower[step][depth, part, :, HALF * t : HALF * t + HALF].astype(f32)


def load_probes(probes, meta, own, near, far):
    core = meta[2 * SLOTS + 2]
    probes[0] = own[...]
    for step in range(1, MODES):
        probes[step, core] = near[step - 1]
        probes[step, 1 - core] = far[step - 1]


def corner_of(meta, turn):
    slot = meta[2 * SLOTS + 1] + MODES * turn
    return meta[2 * slot], meta[2 * slot + 1] - HALF, slot < meta[2 * SLOTS]


def cut(window, patch, row, col):
    keep = lax.broadcasted_iota(jnp.int32, (64, HALF), 1) < HALF - col
    turn = jnp.where(col == 0, 0, HALF - col)
    for part in range(2):
        for block in range(4):
            rows = pl.ds(row + 64 * block, 64)
            rolled = [pltpu.roll(window[part, t, rows], turn, 1) for t in range(3)]
            at = slice(64 * block, 64 * block + 64)
            patch[part, at, 0:HALF] = jnp.where(keep, rolled[0], rolled[1])
            patch[part, at, HALF:PW] = jnp.where(keep, rolled[1], rolled[2])


def place(total, patch, row, col):
    low = lax.broadcasted_iota(jnp.int32, (64, HALF), 1) < col
    zero = jnp.zeros((64, HALF), f32)
    for part in range(2):
        for block in range(4):
            rows = pl.ds(row + 64 * block, 64)
            at = slice(64 * block, 64 * block + 64)
            left = pltpu.roll(patch[part, at, 0:HALF], col, 1)
            right = pltpu.roll(patch[part, at, HALF:PW], col, 1)
            total[part, 0, rows] = total[part, 0, rows] + jnp.where(low, zero, left)
            total[part, 1, rows] = total[part, 1, rows] + jnp.where(low, left, right)
            total[part, 2, rows] = total[part, 2, rows] + jnp.where(low, right, zero)


def share_rows(total, shares, mode):
    for step in range(MODES):
        owner = lax.rem(mode + step, MODES)
        for half in range(2):
            rows = pl.ds(pl.multiple_of(PW * half + SHARE * owner, SHARE), SHARE)
            for part in range(2):
                for t in range(3):
                    shares[step][part, half, t] = total[part, t, rows].astype(bf16)


def set_rows(both, top, bottom):
    both[0:PW] = top.astype(bf16)
    both[PW:] = bottom.astype(bf16)


def set_lanes(both, stacked):
    both[:, 0:PW] = stacked[0:PW].astype(bf16)
    both[:, PW:] = stacked[PW:].astype(bf16)


def each_mode(step):
    def trip(index, _):
        for lane_set in range(UNROLL):
            step(index * UNROLL + lane_set, lane_set)
        return 0

    return lax.fori_loop(0, MODES // UNROLL, trip, 0)


def propagate_kernel(meta, own, east, l0, l1, l2, l3, probe, near, far, left, right, arrived, patches, window, probes, rows, lanes):
    load_probes(probes, meta, probe, near, far)
    build_window(window, 0, meta, own, east, (l0, l1, l2, l3))

    def one_slot(turn, _):
        row, col, _ = corner_of(meta, turn)
        patch = patches.at[turn]
        cut(window, patch, row, col)

        def one_mode(mode, lane_set):
            probe_real, probe_imag = probes[mode, 0].astype(f32), probes[mode, 1].astype(f32)
            real, imag = patch[0], patch[1]
            set_rows(rows.at[lane_set], probe_real * real - probe_imag * imag, probe_real * imag + probe_imag * real)
            set_lanes(lanes.at[lane_set], dot(left[...], rows[lane_set]))
            arrived[turn, mode] = dot(lanes[lane_set], right[...])

        return each_mode(one_mode)

    lax.fori_loop(0, 2, one_slot, 0)


def detector_kernel(meta, own, east, l0, l1, l2, l3, arrived, measured, plus, minus, arrived_grad, g0, g1, g2, g3, window, patch, rows, lanes, far, weight, second, total):
    build_window(window, 1, meta, own, east, (l0, l1, l2, l3))
    total[...] = jnp.zeros_like(total)

    def one_slot(turn, _):
        row, col, live = corner_of(meta, turn)
        cut(window, patch, row, col)

        def forth(mode, lane_set):
            wave_real, wave_imag = arrived[turn, mode, :, 0:PW], arrived[turn, mode, :, PW:]
            real, imag = patch[0], patch[1]
            set_rows(rows.at[lane_set], wave_real * real - wave_imag * imag, wave_real * imag + wave_imag * real)
            set_lanes(lanes.at[lane_set], dot(plus[...], rows[lane_set]))
            field = dot(lanes[lane_set], minus[...])
            far[mode] = field
            power = field[:, 0:PW] * field[:, 0:PW] + field[:, PW:] * field[:, PW:]

            @pl.when(mode == 0)
            def _():
                weight[...] = power - measured[turn].astype(f32)

            @pl.when(mode > 0)
            def _():
                weight[...] = weight[...] + power

        each_mode(forth)
        weight[...] = jnp.where(live, weight[...], 0.0)
        second[...] = jnp.zeros_like(second)

        def back(mode, lane_set):
            scale = weight[...]
            set_rows(rows.at[lane_set], scale * far[mode, :, 0:PW], scale * far[mode, :, PW:])
            set_lanes(lanes.at[lane_set], dot(minus[...], rows[lane_set]))
            leaving = dot(lanes[lane_set], plus[...])
            grad_real, grad_imag = leaving[:, 0:PW], leaving[:, PW:]
            wave_real, wave_imag = arrived[turn, mode, :, 0:PW], arrived[turn, mode, :, PW:]
            second[0] = second[0] + (wave_real * grad_real + wave_imag * grad_imag)
            second[1] = second[1] + (wave_real * grad_imag - wave_imag * grad_real)
            real, imag = patch[0], patch[1]
            arrived_grad[turn, mode, 0:PW] = (real * grad_real + imag * grad_imag).astype(bf16)
            arrived_grad[turn, mode, PW:] = (real * grad_imag - imag * grad_real).astype(bf16)

        each_mode(back)
        place(total, second, row, col)
        return 0

    lax.fori_loop(0, 2, one_slot, 0)
    share_rows(total, (g0, g1, g2, g3), meta[2 * SLOTS + 1])


def return_kernel(meta, patches, arrived_grad, probe, near, far, left, right, g0, g1, g2, g3, kept, sent, probes, lanes, first, total, probe_total):
    load_probes(probes, meta, probe, near, far)
    total[...] = jnp.zeros_like(total)
    probe_total[...] = jnp.zeros_like(probe_total)

    def one_slot(turn, _):
        row, col, _ = corner_of(meta, turn)
        patch = patches.at[turn]
        first[...] = jnp.zeros_like(first)

        def one_mode(mode, lane_set):
            set_lanes(lanes.at[lane_set], dot(left[...], arrived_grad[turn, mode]))
            grad = dot(lanes[lane_set], right[...])
            grad_real, grad_imag = grad[:, 0:PW], grad[:, PW:]
            probe_real, probe_imag = probes[mode, 0].astype(f32), probes[mode, 1].astype(f32)
            real, imag = patch[0], patch[1]
            first[0] = first[0] + (probe_real * grad_real + probe_imag * grad_imag)
            first[1] = first[1] + (probe_real * grad_imag - probe_imag * grad_real)
            probe_total[0, mode] = probe_total[0, mode] + (real * grad_real + imag * grad_imag)
            probe_total[1, mode] = probe_total[1, mode] + (real * grad_imag - imag * grad_real)

        each_mode(one_mode)
        place(total, first, row, col)
        return 0

    lax.fori_loop(0, 2, one_slot, 0)
    share_rows(total, (g0, g1, g2, g3), meta[2 * SLOTS + 1])
    core = meta[2 * SLOTS + 2]
    kept[...] = probe_total[core]
    sent[...] = probe_total[1 - core].astype(bf16)


def kernel_call(body, out_shape, scratch, operands, flops, limit):
    vmem = pl.BlockSpec(memory_space=pltpu.VMEM)
    smem = pl.BlockSpec(memory_space=pltpu.SMEM)
    return pl.pallas_call(
        body,
        out_shape=tuple(jax.ShapeDtypeStruct(*shape) for shape in out_shape),
        in_specs=[smem] + [vmem] * (len(operands) - 1),
        out_specs=tuple(vmem for _ in out_shape),
        scratch_shapes=[pltpu.VMEM(*shape) for shape in scratch],
        compiler_params=pltpu.CompilerParams(vmem_limit_bytes=limit << 20),
        cost_estimate=pl.CostEstimate(flops=flops, bytes_accessed=12 << 20, transcendentals=0),
    )(*operands)


WINDOW = ((2, 3, 2 * PW, HALF), f32)
PATCH = ((2, PW, PW), f32)
ROWS = ((UNROLL, 2 * PW, PW), bf16)
LANES = ((UNROLL, PW, 2 * PW), bf16)
PROBES = ((MODES, 2, PW, PW), bf16)
SHARES = [((2, 2, 3, SHARE, HALF), bf16)] * MODES
TRANSFORM = 8 * 16 * PW * PW * PW


def kernels(meta, pieces, all_probes, turns, matrices):
    plus, minus, left, right = matrices
    arrived, patches = kernel_call(
        propagate_kernel,
        [((2, MODES, PW, 2 * PW), f32), ((2, 2, PW, PW), f32)],
        [WINDOW, PROBES, ROWS, LANES],
        (meta, *pieces, *all_probes, left, right),
        TRANSFORM,
        16,
    )
    arrived_grad, *second_shares = kernel_call(
        detector_kernel,
        [((2, MODES, 2 * PW, PW), bf16)] + SHARES,
        [WINDOW, PATCH, ROWS, LANES, ((MODES, PW, 2 * PW), f32), ((PW, PW), f32), PATCH, WINDOW],
        (meta, *pieces, arrived, turns, plus, minus),
        2 * TRANSFORM,
        26,
    )
    *first_shares, kept, sent = kernel_call(
        return_kernel,
        SHARES + [((MODES, PW, PW), f32), ((MODES, PW, PW), bf16)],
        [PROBES, LANES, PATCH, WINDOW, ((2, MODES, PW, PW), f32)],
        (meta, patches, arrived_grad, *all_probes, right, left),
        TRANSFORM,
        20,
    )
    return second_shares, first_shares, kept, sent


def toward(value, steps):
    pairs = [(t, t + steps) for t in range(TILES) if 0 <= t + steps < TILES]
    return lax.ppermute(value, "tile", pairs)


def to_mode(value, steps):
    return lax.ppermute(value, "mode", [(m, (m + steps) % MODES) for m in range(MODES)])


def tile_of(x, z, core):
    return (x * 8 + z) * 2 + core


def to_core(value):
    return lax.ppermute(value, "tile", [(t, t ^ 1) for t in range(TILES)])


def send_rows(shares):
    received = [shares[0]]
    for step in range(1, MODES):
        received.append(to_mode(shares[step], step))
    return received


def fetch(value):
    received = []
    for step in range(1, MODES):
        received.append(to_mode(value, MODES - step))
    return received


def add_up(values):
    total = values[0].astype(f32)
    for value in values[1:]:
        total = total + value.astype(f32)
    return total


def exchange(value):
    groups = [[tile_of(x, z, c) for x in range(4) for z in range(8)] for c in range(2)]
    return lax.all_to_all(value, "tile", 0, 0, axis_index_groups=groups)


def one_step(object_tiles, probes, measured, offsets, counts):
    tile = lax.axis_index("tile")
    mode = lax.axis_index("mode")
    core = lax.rem(tile, 2)
    own = object_tiles[0]
    quarter = lax.dynamic_slice_in_dim(own, SHARE * mode, SHARE, 2)
    corner = toward(quarter, -TGX - 1)
    south = toward(quarter[..., HALF:], -TGX)
    near = fetch(lax.dynamic_index_in_dim(probes[0], core, 0, keepdims=False).astype(bf16))
    near = jnp.stack(near)
    far = to_core(near)
    east = toward(own, -1)
    lower = jnp.concatenate([south, corner], axis=-1)
    quarters = [lower] + fetch(lower)
    pieces = (own, east, *quarters)
    probe = probes[0].astype(bf16)
    matrices = block_forms(*lax.optimization_barrier(tuple(jnp.asarray(table) for table in constants())))
    meta = jnp.concatenate([offsets.reshape(-1), counts, jnp.stack([mode, core])]).astype(jnp.int32)
    turns = lax.dynamic_index_in_dim(measured[0].reshape(2, MODES, PW, PW), mode, 1, keepdims=False)
    all_probes = (probe, near, far)
    second_shares, first_shares, kept, sent = kernels(meta, pieces, all_probes, turns, matrices)
    second = add_up(send_rows(second_shares))
    halves = kept + to_core(sent).astype(f32)
    mine = add_up(send_rows([halves[0]] + [halves[step].astype(bf16) for step in range(1, MODES)]))
    parts = exchange(mine.astype(bf16).reshape(32, 8, PW))
    part = jnp.sum(parts.astype(f32), axis=0).astype(bf16)
    first = add_up(send_rows(first_shares))
    rows = jnp.stack([first, second])
    upper = rows[:, :, 0] + toward(rows[:, :, 1].astype(bf16), TGX).astype(f32)
    eastward = toward(upper[:, :, 1:].astype(bf16), 1).astype(f32)
    object_grad = jnp.concatenate([eastward[:, :, 0], eastward[:, :, 1] + upper[:, :, 0]], axis=-1)
    plane = exchange(jnp.broadcast_to(part[None], (32, 8, PW))).reshape(PW, PW)
    other = to_core(plane)
    mine_first = (jnp.arange(2, dtype=jnp.int32) == core)[:, None, None]
    probe_grad = jnp.where(mine_first, plane[None].astype(f32), other[None].astype(f32))
    return (object_grad[None], probe_grad[None])


def solution(mesh):
    placed = (
        P("tile", None, None, None, None),
        P("mode", None, None, None),
        P("tile", None, None, None),
        P("tile", None, None),
        P("tile"),
    )
    return jax.shard_map(
        one_step,
        mesh=mesh,
        in_specs=placed,
        out_specs=(P("tile", None, None, "mode", None), P("mode", None, None, None)),
        check_vma=False,
    )
```

```python
import math

import jax
import jax.numpy as jnp
import numpy as np
from jax import lax
from jax.experimental import pallas as pl
from jax.experimental.pallas import tpu as pltpu
from jax.sharding import PartitionSpec as P


PW = 256
HALF = 128
SLOTS = 8
MODES = 4
TGX = 8
TILES = 64
SHARE = PW // MODES
UNROLL = 4
f32 = jnp.float32
bf16 = jnp.bfloat16


def constants():
    indices = np.arange(PW)
    angles = ((indices[:, None] * indices[None, :]) % PW) * (2.0 * math.pi / PW)
    cosine = (np.cos(angles) / math.sqrt(PW)).astype(bf16)
    sine = (np.sin(angles) / math.sqrt(PW)).astype(bf16)
    frequency = (((indices + PW // 2) % PW) - PW // 2) / PW
    phase = np.exp(-1j * math.pi * (PW / 8.0) * frequency * frequency)
    table = cosine.astype(np.float64) - 1j * sine.astype(np.float64)
    hop = np.conj(table) @ (phase[:, None] * table)
    hop_real = hop.real.astype(bf16)
    hop_imag = hop.imag.astype(bf16)
    return cosine, sine, -sine, hop_real, hop_imag, -hop_imag


def block_forms(cosine, sine, minus_sine, hop_real, hop_imag, minus_imag):
    return (
        jnp.block([[cosine, sine], [minus_sine, cosine]]),
        jnp.block([[cosine, minus_sine], [sine, cosine]]),
        jnp.block([[hop_real, minus_imag], [hop_imag, hop_real]]),
        jnp.block([[hop_real, hop_imag], [minus_imag, hop_real]]),
    )


def dot(left, right):
    return jnp.dot(left, right, preferred_element_type=f32)


def build_window(window, depth, meta, own, east, lower):
    for part in range(2):
        window[part, 0, 0:PW] = own[depth, part, :, HALF:].astype(f32)
        for lane_tile in range(2):
            lanes = slice(HALF * lane_tile, HALF * lane_tile + HALF)
            window[part, 1 + lane_tile, 0:PW] = east[part, :, lanes].astype(f32)
        for step in range(MODES):
            owner = lax.rem(meta[2 * SLOTS + 1] + step, MODES)
            rows = pl.ds(pl.multiple_of(PW + SHARE * owner, SHARE), SHARE)
            for t in range(3):
                window[part, t, rows] = lower[step][depth, part, :, HALF * t : HALF * t + HALF].astype(f32)


def load_probes(probes, meta, own, near, far):
    core = meta[2 * SLOTS + 2]
    probes[0] = own[...]
    for step in range(1, MODES):
        probes[step, core] = near[step - 1]
        probes[step, 1 - core] = far[step - 1]


def corner_of(meta, turn):
    slot = meta[2 * SLOTS + 1] + MODES * turn
    return meta[2 * slot], meta[2 * slot + 1] - HALF, slot < meta[2 * SLOTS]


def cut(window, patch, row, col):
    keep = lax.broadcasted_iota(jnp.int32, (64, HALF), 1) < HALF - col
    turn = jnp.where(col == 0, 0, HALF - col)
    for part in range(2):
        for block in range(4):
            rows = pl.ds(row + 64 * block, 64)
            rolled = [pltpu.roll(window[part, t, rows], turn, 1) for t in range(3)]
            at = slice(64 * block, 64 * block + 64)
            patch[part, at, 0:HALF] = jnp.where(keep, rolled[0], rolled[1])
            patch[part, at, HALF:PW] = jnp.where(keep, rolled[1], rolled[2])


def place(total, patch, row, col):
    low = lax.broadcasted_iota(jnp.int32, (64, HALF), 1) < col
    zero = jnp.zeros((64, HALF), f32)
    for part in range(2):
        for block in range(4):
            rows = pl.ds(row + 64 * block, 64)
            at = slice(64 * block, 64 * block + 64)
            left = pltpu.roll(patch[part, at, 0:HALF], col, 1)
            right = pltpu.roll(patch[part, at, HALF:PW], col, 1)
            total[part, 0, rows] = total[part, 0, rows] + jnp.where(low, zero, left)
            total[part, 1, rows] = total[part, 1, rows] + jnp.where(low, left, right)
            total[part, 2, rows] = total[part, 2, rows] + jnp.where(low, right, zero)


def share_rows(total, shares, mode):
    for step in range(MODES):
        owner = lax.rem(mode + step, MODES)
        for half in range(2):
            rows = pl.ds(pl.multiple_of(PW * half + SHARE * owner, SHARE), SHARE)
            for part in range(2):
                for t in range(3):
                    shares[step][part, half, t] = total[part, t, rows].astype(bf16)


def set_rows(both, top, bottom):
    both[0:PW] = top.astype(bf16)
    both[PW:] = bottom.astype(bf16)


def set_lanes(both, stacked):
    both[:, 0:PW] = stacked[0:PW].astype(bf16)
    both[:, PW:] = stacked[PW:].astype(bf16)


def each_mode(step):
    def trip(index, _):
        for lane_set in range(UNROLL):
            step(index * UNROLL + lane_set, lane_set)
        return 0

    return lax.fori_loop(0, MODES // UNROLL, trip, 0)


def propagate_kernel(meta, own, east, l0, l1, l2, l3, probe, near, far, left, right, arrived, patches, window, probes, rows, lanes):
    load_probes(probes, meta, probe, near, far)
    build_window(window, 0, meta, own, east, (l0, l1, l2, l3))

    def one_slot(turn, _):
        row, col, _ = corner_of(meta, turn)
        patch = patches.at[turn]
        cut(window, patch, row, col)

        def one_mode(mode, lane_set):
            probe_real, probe_imag = probes[mode, 0].astype(f32), probes[mode, 1].astype(f32)
            real, imag = patch[0], patch[1]
            set_rows(rows.at[lane_set], probe_real * real - probe_imag * imag, probe_real * imag + probe_imag * real)
            set_lanes(lanes.at[lane_set], dot(left[...], rows[lane_set]))
            arrived[turn, mode] = dot(lanes[lane_set], right[...])

        return each_mode(one_mode)

    lax.fori_loop(0, 2, one_slot, 0, unroll=True)


def detector_kernel(meta, own, east, l0, l1, l2, l3, arrived, measured, plus, minus, arrived_grad, g0, g1, g2, g3, window, patch, rows, lanes, far, weight, second, total):
    build_window(window, 1, meta, own, east, (l0, l1, l2, l3))
    total[...] = jnp.zeros_like(total)

    def one_slot(turn, _):
        row, col, live = corner_of(meta, turn)
        cut(window, patch, row, col)

        def forth(mode, lane_set):
            wave_real, wave_imag = arrived[turn, mode, :, 0:PW], arrived[turn, mode, :, PW:]
            real, imag = patch[0], patch[1]
            set_rows(rows.at[lane_set], wave_real * real - wave_imag * imag, wave_real * imag + wave_imag * real)
            set_lanes(lanes.at[lane_set], dot(plus[...], rows[lane_set]))
            field = dot(lanes[lane_set], minus[...])
            far[mode] = field
            power = field[:, 0:PW] * field[:, 0:PW] + field[:, PW:] * field[:, PW:]

            @pl.when(mode == 0)
            def _():
                weight[...] = power - measured[turn].astype(f32)

            @pl.when(mode > 0)
            def _():
                weight[...] = weight[...] + power

        each_mode(forth)
        weight[...] = jnp.where(live, weight[...], 0.0)
        second[...] = jnp.zeros_like(second)

        def back(mode, lane_set):
            scale = weight[...]
            set_rows(rows.at[lane_set], scale * far[mode, :, 0:PW], scale * far[mode, :, PW:])
            set_lanes(lanes.at[lane_set], dot(minus[...], rows[lane_set]))
            leaving = dot(lanes[lane_set], plus[...])
            grad_real, grad_imag = leaving[:, 0:PW], leaving[:, PW:]
            wave_real, wave_imag = arrived[turn, mode, :, 0:PW], arrived[turn, mode, :, PW:]
            second[0] = second[0] + (wave_real * grad_real + wave_imag * grad_imag)
            second[1] = second[1] + (wave_real * grad_imag - wave_imag * grad_real)
            real, imag = patch[0], patch[1]
            arrived_grad[turn, mode, 0:PW] = (real * grad_real + imag * grad_imag).astype(bf16)
            arrived_grad[turn, mode, PW:] = (real * grad_imag - imag * grad_real).astype(bf16)

        each_mode(back)
        place(total, second, row, col)
        return 0

    lax.fori_loop(0, 2, one_slot, 0)
    share_rows(total, (g0, g1, g2, g3), meta[2 * SLOTS + 1])


def return_kernel(meta, patches, arrived_grad, probe, near, far, left, right, g0, g1, g2, g3, kept, sent, probes, lanes, first, total, probe_total):
    load_probes(probes, meta, probe, near, far)
    total[...] = jnp.zeros_like(total)
    probe_total[...] = jnp.zeros_like(probe_total)

    def one_slot(turn, _):
        row, col, _ = corner_of(meta, turn)
        patch = patches.at[turn]
        first[...] = jnp.zeros_like(first)

        def one_mode(mode, lane_set):
            set_lanes(lanes.at[lane_set], dot(left[...], arrived_grad[turn, mode]))
            grad = dot(lanes[lane_set], right[...])
            grad_real, grad_imag = grad[:, 0:PW], grad[:, PW:]
            probe_real, probe_imag = probes[mode, 0].astype(f32), probes[mode, 1].astype(f32)
            real, imag = patch[0], patch[1]
            first[0] = first[0] + (probe_real * grad_real + probe_imag * grad_imag)
            first[1] = first[1] + (probe_real * grad_imag - probe_imag * grad_real)
            probe_total[0, mode] = probe_total[0, mode] + (real * grad_real + imag * grad_imag)
            probe_total[1, mode] = probe_total[1, mode] + (real * grad_imag - imag * grad_real)

        each_mode(one_mode)
        place(total, first, row, col)
        return 0

    lax.fori_loop(0, 2, one_slot, 0, unroll=True)
    share_rows(total, (g0, g1, g2, g3), meta[2 * SLOTS + 1])
    core = meta[2 * SLOTS + 2]
    kept[...] = probe_total[core]
    sent[...] = probe_total[1 - core].astype(bf16)


def kernel_call(body, out_shape, scratch, operands, flops, limit):
    vmem = pl.BlockSpec(memory_space=pltpu.VMEM)
    smem = pl.BlockSpec(memory_space=pltpu.SMEM)
    return pl.pallas_call(
        body,
        out_shape=tuple(jax.ShapeDtypeStruct(*shape) for shape in out_shape),
        in_specs=[smem] + [vmem] * (len(operands) - 1),
        out_specs=tuple(vmem for _ in out_shape),
        scratch_shapes=[pltpu.VMEM(*shape) for shape in scratch],
        compiler_params=pltpu.CompilerParams(vmem_limit_bytes=limit << 20),
        cost_estimate=pl.CostEstimate(flops=flops, bytes_accessed=12 << 20, transcendentals=0),
    )(*operands)


WINDOW = ((2, 3, 2 * PW, HALF), f32)
PATCH = ((2, PW, PW), f32)
ROWS = ((UNROLL, 2 * PW, PW), bf16)
LANES = ((UNROLL, PW, 2 * PW), bf16)
PROBES = ((MODES, 2, PW, PW), bf16)
SHARES = [((2, 2, 3, SHARE, HALF), bf16)] * MODES
TRANSFORM = 8 * 16 * PW * PW * PW


def kernels(meta, pieces, all_probes, turns, matrices):
    plus, minus, left, right = matrices
    own, east_one, east_two, *quarters = pieces
    arrived, patches = kernel_call(
        propagate_kernel,
        [((2, MODES, PW, 2 * PW), f32), ((2, 2, PW, PW), f32)],
        [WINDOW, PROBES, ROWS, LANES],
        (meta, own, east_one, *quarters, *all_probes, left, right),
        TRANSFORM,
        16,
    )
    arrived_grad, *second_shares = kernel_call(
        detector_kernel,
        [((2, MODES, 2 * PW, PW), bf16)] + SHARES,
        [WINDOW, PATCH, ROWS, LANES, ((MODES, PW, 2 * PW), f32), ((PW, PW), f32), PATCH, WINDOW],
        (meta, own, east_two, *quarters, arrived, turns, plus, minus),
        2 * TRANSFORM,
        26,
    )
    *first_shares, kept, sent = kernel_call(
        return_kernel,
        SHARES + [((MODES, PW, PW), f32), ((MODES, PW, PW), bf16)],
        [PROBES, LANES, PATCH, WINDOW, ((2, MODES, PW, PW), f32)],
        (meta, patches, arrived_grad, *all_probes, right, left),
        TRANSFORM,
        20,
    )
    return second_shares, first_shares, kept, sent


def toward(value, steps):
    pairs = [(t, t + steps) for t in range(TILES) if 0 <= t + steps < TILES]
    return lax.ppermute(value, "tile", pairs)


def to_mode(value, steps):
    return lax.ppermute(value, "mode", [(m, (m + steps) % MODES) for m in range(MODES)])


def tile_of(x, z, core):
    return (x * 8 + z) * 2 + core


def to_core(value):
    return lax.ppermute(value, "tile", [(t, t ^ 1) for t in range(TILES)])


def send_rows(shares):
    received = [shares[0]]
    for step in range(1, MODES):
        received.append(to_mode(shares[step], step))
    return received


def fetch(value):
    received = []
    for step in range(1, MODES):
        received.append(to_mode(value, MODES - step))
    return received


def add_up(values):
    total = values[0].astype(f32)
    for value in values[1:]:
        total = total + value.astype(f32)
    return total


def exchange(value):
    groups = [[tile_of(x, z, c) for x in range(4) for z in range(8)] for c in range(2)]
    return lax.all_to_all(value, "tile", 0, 0, axis_index_groups=groups)


def one_step(object_tiles, probes, measured, offsets, counts):
    tile = lax.axis_index("tile")
    mode = lax.axis_index("mode")
    core = lax.rem(tile, 2)
    own = object_tiles[0]
    quarter = lax.dynamic_slice_in_dim(own, SHARE * mode, SHARE, 2)
    corner = toward(quarter, -TGX - 1)
    south = toward(quarter[..., HALF:], -TGX)
    near = fetch(lax.dynamic_index_in_dim(probes[0], core, 0, keepdims=False).astype(bf16))
    near = jnp.stack(near)
    far = to_core(near)
    east_one = toward(own[0], -1)
    east_two = toward(own[1], -1)
    lower = jnp.concatenate([south, corner], axis=-1)
    quarters = [lower] + fetch(lower)
    pieces = (own, east_one, east_two, *quarters)
    probe = probes[0].astype(bf16)
    matrices = block_forms(*lax.optimization_barrier(tuple(jnp.asarray(table) for table in constants())))
    meta = jnp.concatenate([offsets.reshape(-1), counts, jnp.stack([mode, core])]).astype(jnp.int32)
    turns = lax.dynamic_index_in_dim(measured[0].reshape(2, MODES, PW, PW), mode, 1, keepdims=False)
    all_probes = (probe, near, far)
    second_shares, first_shares, kept, sent = kernels(meta, pieces, all_probes, turns, matrices)
    second = add_up(send_rows(second_shares))
    halves = kept + to_core(sent).astype(f32)
    mine = add_up(send_rows([halves[0]] + [halves[step].astype(bf16) for step in range(1, MODES)]))
    parts = exchange(mine.astype(bf16).reshape(32, 8, PW))
    part = jnp.sum(parts.astype(f32), axis=0).astype(bf16)
    first = add_up(send_rows(first_shares))
    rows = jnp.stack([first, second])
    upper = rows[:, :, 0] + toward(rows[:, :, 1].astype(bf16), TGX).astype(f32)
    eastward = toward(upper[:, :, 1:].astype(bf16), 1).astype(f32)
    object_grad = jnp.concatenate([eastward[:, :, 0], eastward[:, :, 1] + upper[:, :, 0]], axis=-1)
    plane = exchange(jnp.broadcast_to(part[None], (32, 8, PW))).reshape(PW, PW)
    other = to_core(plane)
    mine_first = (jnp.arange(2, dtype=jnp.int32) == core)[:, None, None]
    probe_grad = jnp.where(mine_first, plane[None].astype(f32), other[None].astype(f32))
    return (object_grad[None], probe_grad[None])


def solution(mesh):
    placed = (
        P("tile", None, None, None, None),
        P("mode", None, None, None),
        P("tile", None, None, None),
        P("tile", None, None),
        P("tile"),
    )
    return jax.shard_map(
        one_step,
        mesh=mesh,
        in_specs=placed,
        out_specs=(P("tile", None, None, "mode", None), P("mode", None, None, None)),
        check_vma=False,
    )
```

```python
import math

import jax
import jax.numpy as jnp
import numpy as np
from jax import lax
from jax.experimental import pallas as pl
from jax.experimental.pallas import tpu as pltpu
from jax.sharding import PartitionSpec as P


PW = 256
HALF = 128
SLOTS = 8
MODES = 4
TGX = 8
TILES = 64
SHARE = PW // MODES
UNROLL = 4
f32 = jnp.float32
bf16 = jnp.bfloat16


def constants():
    indices = np.arange(PW)
    angles = ((indices[:, None] * indices[None, :]) % PW) * (2.0 * math.pi / PW)
    cosine = (np.cos(angles) / math.sqrt(PW)).astype(bf16)
    sine = (np.sin(angles) / math.sqrt(PW)).astype(bf16)
    frequency = (((indices + PW // 2) % PW) - PW // 2) / PW
    phase = np.exp(-1j * math.pi * (PW / 8.0) * frequency * frequency)
    table = cosine.astype(np.float64) - 1j * sine.astype(np.float64)
    hop = np.conj(table) @ (phase[:, None] * table)
    hop_real = hop.real.astype(bf16)
    hop_imag = hop.imag.astype(bf16)
    return cosine, sine, -sine, hop_real, hop_imag, -hop_imag


def block_forms(cosine, sine, minus_sine, hop_real, hop_imag, minus_imag):
    return (
        jnp.block([[cosine, sine], [minus_sine, cosine]]),
        jnp.block([[cosine, minus_sine], [sine, cosine]]),
        jnp.block([[hop_real, minus_imag], [hop_imag, hop_real]]),
        jnp.block([[hop_real, hop_imag], [minus_imag, hop_real]]),
    )


def dot(left, right):
    return jnp.dot(left, right, preferred_element_type=f32)


def build_window(window, depth, meta, own, east, lower):
    for part in range(2):
        window[part, 0, 0:PW] = own[depth, part, :, HALF:].astype(f32)
        for lane_tile in range(2):
            lanes = slice(HALF * lane_tile, HALF * lane_tile + HALF)
            window[part, 1 + lane_tile, 0:PW] = east[depth, part, :, lanes].astype(f32)
        for step in range(MODES):
            owner = lax.rem(meta[2 * SLOTS + 1] + step, MODES)
            rows = pl.ds(pl.multiple_of(PW + SHARE * owner, SHARE), SHARE)
            for t in range(3):
                window[part, t, rows] = lower[step][depth, part, :, HALF * t : HALF * t + HALF].astype(f32)


def load_probes(probes, meta, own, near, far):
    core = meta[2 * SLOTS + 2]
    probes[0] = own[...].astype(bf16)
    for step in range(1, MODES):
        probes[step, core] = near[step - 1]
        probes[step, 1 - core] = far[step - 1]


def corner_of(meta, turn):
    slot = meta[2 * SLOTS + 1] + MODES * turn
    return meta[slot], meta[SLOTS + slot] - HALF, slot < meta[2 * SLOTS]


def cut(window, patch, row, col):
    keep = lax.broadcasted_iota(jnp.int32, (64, HALF), 1) < HALF - col
    turn = jnp.where(col == 0, 0, HALF - col)
    for part in range(2):
        for block in range(4):
            rows = pl.ds(row + 64 * block, 64)
            rolled = [pltpu.roll(window[part, t, rows], turn, 1) for t in range(3)]
            at = slice(64 * block, 64 * block + 64)
            patch[part, at, 0:HALF] = jnp.where(keep, rolled[0], rolled[1])
            patch[part, at, HALF:PW] = jnp.where(keep, rolled[1], rolled[2])


def place(total, patch, row, col):
    low = lax.broadcasted_iota(jnp.int32, (64, HALF), 1) < col
    zero = jnp.zeros((64, HALF), f32)
    for part in range(2):
        for block in range(4):
            rows = pl.ds(row + 64 * block, 64)
            at = slice(64 * block, 64 * block + 64)
            left = pltpu.roll(patch[part, at, 0:HALF], col, 1)
            right = pltpu.roll(patch[part, at, HALF:PW], col, 1)
            total[part, 0, rows] = total[part, 0, rows] + jnp.where(low, zero, left)
            total[part, 1, rows] = total[part, 1, rows] + jnp.where(low, left, right)
            total[part, 2, rows] = total[part, 2, rows] + jnp.where(low, right, zero)


def share_rows(total, shares, mode):
    for step in range(MODES):
        owner = lax.rem(mode + step, MODES)
        for half in range(2):
            rows = pl.ds(pl.multiple_of(PW * half + SHARE * owner, SHARE), SHARE)
            for part in range(2):
                for t in range(3):
                    shares[step][part, half, t] = total[part, t, rows].astype(bf16)


def set_rows(both, top, bottom):
    both[0:PW] = top.astype(bf16)
    both[PW:] = bottom.astype(bf16)


def set_lanes(both, stacked):
    both[:, 0:PW] = stacked[0:PW].astype(bf16)
    both[:, PW:] = stacked[PW:].astype(bf16)


def each_mode(step):
    def trip(index, _):
        for lane_set in range(UNROLL):
            step(index * UNROLL + lane_set, lane_set)
        return 0

    return lax.fori_loop(0, MODES // UNROLL, trip, 0)


def propagate_kernel(meta, own, east, l0, l1, l2, l3, probe, near, far, left, right, arrived, patches, window, probes, rows, lanes):
    load_probes(probes, meta, probe, near, far)
    build_window(window, 0, meta, own, east, (l0, l1, l2, l3))

    def one_slot(turn, _):
        row, col, _ = corner_of(meta, turn)
        patch = patches.at[turn]
        cut(window, patch, row, col)

        def one_mode(mode, lane_set):
            probe_real, probe_imag = probes[mode, 0].astype(f32), probes[mode, 1].astype(f32)
            real, imag = patch[0], patch[1]
            set_rows(rows.at[lane_set], probe_real * real - probe_imag * imag, probe_real * imag + probe_imag * real)
            set_lanes(lanes.at[lane_set], dot(left[...], rows[lane_set]))
            arrived[turn, mode] = dot(lanes[lane_set], right[...])

        return each_mode(one_mode)

    lax.fori_loop(0, 2, one_slot, 0, unroll=True)


def detector_kernel(meta, own, east, l0, l1, l2, l3, arrived, measured, plus, minus, arrived_grad, g0, g1, g2, g3, window, patch, rows, lanes, far, weight, second, total):
    build_window(window, 1, meta, own, east, (l0, l1, l2, l3))
    total[...] = jnp.zeros_like(total)

    def one_slot(turn, _):
        row, col, live = corner_of(meta, turn)
        cut(window, patch, row, col)

        def forth(mode, lane_set):
            wave_real, wave_imag = arrived[turn, mode, :, 0:PW], arrived[turn, mode, :, PW:]
            real, imag = patch[0], patch[1]
            set_rows(rows.at[lane_set], wave_real * real - wave_imag * imag, wave_real * imag + wave_imag * real)
            set_lanes(lanes.at[lane_set], dot(plus[...], rows[lane_set]))
            field = dot(lanes[lane_set], minus[...])
            far[mode] = field
            power = field[:, 0:PW] * field[:, 0:PW] + field[:, PW:] * field[:, PW:]

            @pl.when(mode == 0)
            def _():
                weight[...] = power - measured[turn].astype(f32)

            @pl.when(mode > 0)
            def _():
                weight[...] = weight[...] + power

        each_mode(forth)
        weight[...] = jnp.where(live, weight[...], 0.0)
        second[...] = jnp.zeros_like(second)

        def back(mode, lane_set):
            scale = weight[...]
            set_rows(rows.at[lane_set], scale * far[mode, :, 0:PW], scale * far[mode, :, PW:])
            set_lanes(lanes.at[lane_set], dot(minus[...], rows[lane_set]))
            leaving = dot(lanes[lane_set], plus[...])
            grad_real, grad_imag = leaving[:, 0:PW], leaving[:, PW:]
            wave_real, wave_imag = arrived[turn, mode, :, 0:PW], arrived[turn, mode, :, PW:]
            second[0] = second[0] + (wave_real * grad_real + wave_imag * grad_imag)
            second[1] = second[1] + (wave_real * grad_imag - wave_imag * grad_real)
            real, imag = patch[0], patch[1]
            arrived_grad[turn, mode, 0:PW] = (real * grad_real + imag * grad_imag).astype(bf16)
            arrived_grad[turn, mode, PW:] = (real * grad_imag - imag * grad_real).astype(bf16)

        each_mode(back)
        place(total, second, row, col)
        return 0

    lax.fori_loop(0, 2, one_slot, 0, unroll=True)
    share_rows(total, (g0, g1, g2, g3), meta[2 * SLOTS + 1])


def return_kernel(meta, patches, arrived_grad, probe, near, far, left, right, g0, g1, g2, g3, kept, sent, probes, lanes, first, total, probe_total):
    load_probes(probes, meta, probe, near, far)
    total[...] = jnp.zeros_like(total)
    probe_total[...] = jnp.zeros_like(probe_total)

    def one_slot(turn, _):
        row, col, _ = corner_of(meta, turn)
        patch = patches.at[turn]
        first[...] = jnp.zeros_like(first)

        def one_mode(mode, lane_set):
            set_lanes(lanes.at[lane_set], dot(left[...], arrived_grad[turn, mode]))
            grad = dot(lanes[lane_set], right[...])
            grad_real, grad_imag = grad[:, 0:PW], grad[:, PW:]
            probe_real, probe_imag = probes[mode, 0].astype(f32), probes[mode, 1].astype(f32)
            real, imag = patch[0], patch[1]
            first[0] = first[0] + (probe_real * grad_real + probe_imag * grad_imag)
            first[1] = first[1] + (probe_real * grad_imag - probe_imag * grad_real)
            probe_total[0, mode] = probe_total[0, mode] + (real * grad_real + imag * grad_imag)
            probe_total[1, mode] = probe_total[1, mode] + (real * grad_imag - imag * grad_real)

        each_mode(one_mode)
        place(total, first, row, col)
        return 0

    lax.fori_loop(0, 2, one_slot, 0, unroll=True)
    share_rows(total, (g0, g1, g2, g3), meta[2 * SLOTS + 1])
    core = meta[2 * SLOTS + 2]
    kept[...] = probe_total[core]
    sent[...] = probe_total[1 - core].astype(bf16)


def kernel_call(body, out_shape, scratch, operands, flops, limit):
    vmem = pl.BlockSpec(memory_space=pltpu.VMEM)
    smem = pl.BlockSpec(memory_space=pltpu.SMEM)
    return pl.pallas_call(
        body,
        out_shape=tuple(jax.ShapeDtypeStruct(*shape) for shape in out_shape),
        in_specs=[smem] + [vmem] * (len(operands) - 1),
        out_specs=tuple(vmem for _ in out_shape),
        scratch_shapes=[pltpu.VMEM(*shape) for shape in scratch],
        compiler_params=pltpu.CompilerParams(vmem_limit_bytes=limit << 20),
        cost_estimate=pl.CostEstimate(flops=flops, bytes_accessed=12 << 20, transcendentals=0),
    )(*operands)


WINDOW = ((2, 3, 2 * PW, HALF), f32)
PATCH = ((2, PW, PW), f32)
ROWS = ((UNROLL, 2 * PW, PW), bf16)
LANES = ((UNROLL, PW, 2 * PW), bf16)
PROBES = ((MODES, 2, PW, PW), bf16)
SHARES = [((2, 2, 3, SHARE, HALF), bf16)] * MODES
TRANSFORM = 8 * 16 * PW * PW * PW


def kernels(meta, pieces, all_probes, turns, matrices):
    plus, minus, left, right = matrices
    arrived, patches = kernel_call(
        propagate_kernel,
        [((2, MODES, PW, 2 * PW), f32), ((2, 2, PW, PW), f32)],
        [WINDOW, PROBES, ROWS, LANES],
        (meta, *pieces, *all_probes, left, right),
        TRANSFORM,
        16,
    )
    arrived_grad, *second_shares = kernel_call(
        detector_kernel,
        [((2, MODES, 2 * PW, PW), bf16)] + SHARES,
        [WINDOW, PATCH, ROWS, LANES, ((MODES, PW, 2 * PW), f32), ((PW, PW), f32), PATCH, WINDOW],
        (meta, *pieces, arrived, turns, plus, minus),
        2 * TRANSFORM,
        26,
    )
    *first_shares, kept, sent = kernel_call(
        return_kernel,
        SHARES + [((MODES, PW, PW), f32), ((MODES, PW, PW), bf16)],
        [PROBES, LANES, PATCH, WINDOW, ((2, MODES, PW, PW), f32)],
        (meta, patches, arrived_grad, *all_probes, right, left),
        TRANSFORM,
        20,
    )
    return second_shares, first_shares, kept, sent


def toward(value, steps):
    pairs = [(t, t + steps) for t in range(TILES) if 0 <= t + steps < TILES]
    return lax.ppermute(value, "tile", pairs)


def to_mode(value, steps):
    return lax.ppermute(value, "mode", [(m, (m + steps) % MODES) for m in range(MODES)])


def tile_of(x, z, core):
    return (x * 8 + z) * 2 + core


def to_core(value):
    return lax.ppermute(value, "tile", [(t, t ^ 1) for t in range(TILES)])


def send_rows(shares):
    received = [shares[0]]
    for step in range(1, MODES):
        received.append(to_mode(shares[step], step))
    return received


def fetch(value):
    received = []
    for step in range(1, MODES):
        received.append(to_mode(value, MODES - step))
    return received


def add_up(values):
    total = values[0].astype(f32)
    for value in values[1:]:
        total = total + value.astype(f32)
    return total


def exchange(value):
    groups = [[tile_of(x, z, c) for x in range(4) for z in range(8)] for c in range(2)]
    return lax.all_to_all(value, "tile", 0, 0, axis_index_groups=groups)


def one_step(object_tiles, probes, measured, offsets, counts):
    tile = lax.axis_index("tile")
    mode = lax.axis_index("mode")
    core = lax.rem(tile, 2)
    own = object_tiles[0]
    quarter = lax.dynamic_slice_in_dim(own, SHARE * mode, SHARE, 2)
    corner = toward(quarter, -TGX - 1)
    south = toward(quarter[..., HALF:], -TGX)
    near = fetch(lax.dynamic_index_in_dim(probes[0], core, 0, keepdims=False).astype(bf16))
    near = jnp.stack(near)
    far = to_core(near)
    east = toward(own, -1)
    lower = jnp.concatenate([south, corner], axis=-1)
    quarters = [lower] + fetch(lower)
    pieces = (own, east, *quarters)
    matrices = block_forms(*lax.optimization_barrier(tuple(jnp.asarray(table) for table in constants())))
    meta = jnp.concatenate([offsets[0].T.reshape(-1), counts, jnp.stack([mode, core])]).astype(jnp.int32)
    turns = lax.dynamic_index_in_dim(measured[0].reshape(2, MODES, PW, PW), mode, 1, keepdims=False)
    all_probes = (probes[0], near, far)
    second_shares, first_shares, kept, sent = kernels(meta, pieces, all_probes, turns, matrices)
    second = add_up(send_rows(second_shares))
    halves = kept + to_core(sent).astype(f32)
    mine = add_up(send_rows([halves[0]] + [halves[step].astype(bf16) for step in range(1, MODES)]))
    parts = exchange(mine.astype(bf16).reshape(32, 8, PW))
    part = jnp.sum(parts.astype(f32), axis=0).astype(bf16)
    first = add_up(send_rows(first_shares))
    rows = jnp.stack([first, second])
    upper = rows[:, :, 0] + toward(rows[:, :, 1].astype(bf16), TGX).astype(f32)
    eastward = toward(upper[:, :, 1:].astype(bf16), 1).astype(f32)
    object_grad = jnp.concatenate([eastward[:, :, 0], eastward[:, :, 1] + upper[:, :, 0]], axis=-1)
    plane = exchange(jnp.broadcast_to(part[None], (32, 8, PW))).reshape(PW, PW)
    other = to_core(plane)
    mine_first = (jnp.arange(2, dtype=jnp.int32) == core)[:, None, None]
    probe_grad = jnp.where(mine_first, plane[None].astype(f32), other[None].astype(f32))
    return (object_grad[None], probe_grad[None])


def solution(mesh):
    placed = (
        P("tile", None, None, None, None),
        P("mode", None, None, None),
        P("tile", None, None, None),
        P("tile", None, None),
        P("tile"),
    )
    return jax.shard_map(
        one_step,
        mesh=mesh,
        in_specs=placed,
        out_specs=(P("tile", None, None, "mode", None), P("mode", None, None, None)),
        check_vma=False,
    )
```
